32 devices in a mesh: ctx: 8 (over z, y), grp: 4 (over x, core).
Axes of the slice: x: 2, y: 2, z: 4, core: 2. Of those that a mesh axis runs over, the one named last changes fastest.
Arguments:
- streams: bfloat16 [3, 3072, 4096], P(None, 'ctx', 'grp'), may hold values from -400 to 400
- filters: bfloat16 [3, 256, 128], P(None, 'grp'), may hold values from -0.5 to 0.5
- gain: float32 [4096], P('grp'), may hold values from 0.5 to 1.5
Outputs:
- normed: bfloat16 [3072, 4096], P('ctx', 'grp')
The draws below stay inside these ranges and needn't reach their ends.
All inputs are finite; a program needn't handle non-finite values.
Results may differ from the reference program's by a relative error of at most 0.012.
The reference program's roundings to bfloat16 on the way count: a program that leaves them out, or rounds other values in their place, can miss the bound.
Values may be sent and summed in bfloat16 or wider, within the bound.
A program may use at most 128 MiB of HBM per device.

```python
import math
import jax
import jax.numpy as jnp
import numpy as np
from jax import lax

HEADS = 32
HD = 128
FG = 256
FLEN = 128
CH = 4096
LEN = 3072


def draw_streams(key, part):
    key_list = jax.random.split(key, 2)
    base = jnp.clip(jax.random.normal(key_list[0], (3, LEN, CH), jnp.float32), -4.0, 4.0)
    chan_top = 10.0
    chan_scale = jnp.exp(math.log(chan_top) * jnp.arange(CH, dtype=jnp.float32) / (CH - 1))
    tok_scale = jnp.exp(jax.random.uniform(key_list[1], (LEN,), jnp.float32, 0.0, math.log(3.0)))
    base = base.at[2].multiply(tok_scale[:, None] * chan_scale[None, :])
    return base.astype(jnp.bfloat16)


def level_of(own_key, extent, shards, least, largest):
    factor_of = 1.0
    for dim, shards_of in shards:
        draws = jax.random.uniform(jax.random.fold_in(jax.random.fold_in(own_key, 6), dim), (shards_of,), jnp.float32, least / len(shards), largest / len(shards))
        factor_of = factor_of * jnp.repeat(jnp.exp(draws), extent[dim] // shards_of).reshape((-1,) + (1,) * (len(extent) - 1 - dim))
    return factor_of


def scatter_about(stream_key, extent, width, most, shards=(), kind=jnp.bfloat16):
    level = level_of(stream_key, extent, shards, -0.22, 0.18) if shards else 1.0
    values = jax.random.normal(stream_key, extent, jnp.float32) * width * level
    return jnp.minimum(jnp.maximum(values, -most), most).astype(kind)


def setup_inputs(seed: int = 0) -> dict:
    key_of = jax.random.split(jax.random.key(seed), 4)
    return {
        "streams": draw_streams(jax.random.fold_in(key_of[3], 71), 0),
        "filters": scatter_about(key_of[1], (3, FG, FLEN), FLEN ** -0.5, 0.5, ((1, 4),)),
        "gain": jnp.clip(1.0 + 0.1 * jax.random.normal(key_of[2], (CH,), jnp.float32), 0.5, 1.5),
    }


def filter_stream(values, taps):
    group_width = CH // FG
    block_count = LEN // FLEN
    lag_table = np.arange(FLEN)[:, None] - np.arange(FLEN)[None, :]
    lower_idx = np.where(lag_table >= 0, lag_table, 0)
    upper_idx = np.where(lag_table < 0, lag_table + FLEN, 0)
    taps_wide = taps.astype(jnp.float32)
    lower = jnp.where(lag_table >= 0, taps_wide[:, lower_idx], 0.0)
    upper = jnp.where(lag_table < 0, taps_wide[:, upper_idx], 0.0)
    wide = values.astype(jnp.float32)
    padded = jnp.concatenate([jnp.zeros((FLEN, CH), wide.dtype), wide], axis=0)
    blocks = padded.reshape(block_count + 1, FLEN, FG, group_width)
    result = jnp.einsum('gts,bsgc->btgc', lower, blocks[1:], precision=lax.Precision.HIGHEST)
    result = result + jnp.einsum('gts,bsgc->btgc', upper, blocks[:-1], precision=lax.Precision.HIGHEST)
    return result.reshape(LEN, CH).astype(jnp.bfloat16)

def reference(streams, filters, gain):
    features = [filter_stream(streams[idx], filters[idx]) for idx in range(3)]
    split = [feat.reshape(LEN, HEADS, HD).transpose(1, 0, 2) for feat in features]
    block_rows = math.gcd(LEN, 1024)
    outputs = []
    for block_idx in range(LEN // block_rows):
        first = block_idx * block_rows
        key_len = first + block_rows
        query_pos = first + jnp.arange(block_rows, dtype=jnp.int32)
        key_pos = jnp.arange(key_len, dtype=jnp.int32)
        causal = query_pos[:, None] >= key_pos[None, :]

        def head_attention(triple):
            query, keyed, valued = triple
            scores = jnp.dot(query, keyed.T, preferred_element_type=jnp.float32) * HD ** (-0.5)
            top = lax.optimization_barrier(jnp.max(jnp.where(causal, scores, -1e+30), axis=1))
            weights = jnp.where(causal, jnp.exp(scores - top[:, None]), 0.0)
            numer = jnp.dot(weights.astype(jnp.bfloat16), valued, preferred_element_type=jnp.float32)
            return (numer / lax.optimization_barrier(jnp.sum(weights, axis=1))[:, None]).astype(jnp.bfloat16)
        per_head = lax.map(head_attention, (split[0][:, first:key_len], split[1][:, :key_len], split[2][:, :key_len]))
        outputs.append(per_head.transpose(1, 0, 2).reshape(block_rows, CH))
    attended = jnp.concatenate(outputs, axis=0)
    wide = attended.astype(jnp.float32)
    power = lax.optimization_barrier(jnp.mean(wide * wide, axis=1))
    return (wide * gain[None, :] / jnp.sqrt(power + 1e-06)[:, None]).astype(jnp.bfloat16)
```

```python
import functools
import math

import jax
import jax.numpy as jnp
import numpy as np
from jax import lax
from jax.experimental import pallas as pl
from jax.experimental.pallas import tpu as pltpu
from jax.sharding import PartitionSpec as P

HD = 128
LANES = 128
MESH = pl.DeviceIdType.MESH
SIDES = 2
LAYERS = 4
HUB = 1


def layered_kernel(
    n,
    n_grp,
    streams,
    filters,
    gain,
    out,
    buf,
    turned,
    toep,
    feat,
    far_kv,
    far_q,
    part,
    part_stat,
    inbox,
    in_stat,
    own_acc,
    own_top,
    own_total,
    sending,
    att,
    sums,
    local_sem,
    side_send,
    side_recv,
    halo_send,
    halo_recv,
    kv_send,
    kv_recv,
    q_send,
    q_recv,
    part_send,
    part_recv,
    stat_send,
    stat_recv,
    back_send,
    back_recv,
    sum_send,
    sum_recv,
):
    me = lax.axis_index("ctx")
    my_grp = lax.axis_index("grp")
    layer = me // SIDES
    side = lax.rem(me, SIDES)
    other = 1 - side
    rows = streams.shape[1]
    chans = streams.shape[2]
    groups = filters.shape[1]
    flen = filters.shape[2]
    half = chans // SIDES
    heads = half // HD
    span = rows * SIDES
    width = chans // groups
    per_tile = LANES // width
    factor = HD ** (-0.5) * math.log2(math.e)

    def place(z, y):
        return {"ctx": z * SIDES + y}

    def lanes_of(h):
        return pl.ds(pl.multiple_of(h * HD, HD), HD)

    def half_lanes(y, h):
        return pl.ds(pl.multiple_of(y * half + h * HD, HD), HD)

    def remote(src, dst, send, recv, device):
        return pltpu.make_async_remote_copy(
            src_ref=src,
            dst_ref=dst,
            send_sem=send,
            recv_sem=recv,
            device_id=device,
            device_id_type=MESH,
        )

    def own_copy():
        start = pl.multiple_of(flen + side * rows, flen)
        return pltpu.make_async_copy(
            streams.at[:, :, pl.ds(pl.multiple_of(side * half, HD), half)],
            buf.at[:, pl.ds(start, rows), :],
            local_sem.at[0],
        )

    def side_copy(s, h, y):
        start = pl.multiple_of(flen + y * rows, flen)
        return remote(
            streams.at[s, :, half_lanes(1 - y, h)],
            buf.at[s, pl.ds(start, rows), lanes_of(h)],
            side_send.at[s, h],
            side_recv.at[s, h],
            place(layer, other),
        )

    def halo_copy(h, y):
        return remote(
            streams.at[:, pl.ds(rows - flen, flen), half_lanes(y, h)],
            buf.at[:, pl.ds(0, flen), lanes_of(h)],
            halo_send.at[y, h],
            halo_recv.at[h],
            place(lax.rem(layer + 1, LAYERS), y),
        )

    def kv_copy(h):
        return remote(
            feat.at[pl.ds(1, 2), :, lanes_of(h)],
            far_kv.at[:, :, lanes_of(h)],
            kv_send.at[h],
            kv_recv.at[h],
            place(HUB, side),
        )

    def q_copy(d, h):
        return remote(
            feat.at[0, :, lanes_of(h)],
            far_q.at[d, :, lanes_of(h)],
            q_send.at[d, h],
            q_recv.at[d, h],
            place(lax.rem(layer + LAYERS - d - 1, LAYERS), side),
        )

    def part_copy(d, h, r):
        where = pl.ds(r * rows, rows)
        return remote(
            part.at[d, where, lanes_of(h)],
            inbox.at[d, where, lanes_of(h)],
            part_send.at[d, h, r],
            part_recv.at[d, h, r],
            place(lax.rem(layer + d + 1, LAYERS), side),
        )

    def stat_copy(d, h, r):
        return remote(
            part_stat.at[d, h, r],
            in_stat.at[d, h, r],
            stat_send.at[d, h, r],
            stat_recv.at[d, h, r],
            place(lax.rem(layer + d + 1, LAYERS), side),
        )

    def back_copy(h, y):
        return remote(
            sending.at[:, lanes_of(h)],
            att.at[:, half_lanes(y, h)],
            back_send.at[h],
            back_recv.at[h],
            place(layer, other),
        )

    barrier = pltpu.get_barrier_semaphore()
    for k in range(1, n):
        pl.semaphore_signal(
            barrier, inc=1, device_id={"ctx": lax.rem(me + k, n)}, device_id_type=MESH
        )
    for k in range(1, n_grp):
        pl.semaphore_signal(
            barrier, inc=1, device_id={"grp": lax.rem(my_grp + k, n_grp)}, device_id_type=MESH
        )
    own_copy().start()
    pl.semaphore_wait(barrier, n - 1 + n_grp - 1)

    lead = jnp.where(layer <= HUB, 1, 0)

    def stream_at(j):
        return lax.rem(j + lead, 3)

    @pl.loop(0, heads)
    def _(h):
        for j in range(3):
            side_copy(stream_at(j), h, side).start()

        @pl.when((side == SIDES - 1) & (layer < LAYERS - 1))
        def _():
            for y in range(SIDES):
                halo_copy(h, y).start()

    @pl.when(layer == 0)
    def _():
        for s in range(3):
            buf[s, pl.ds(0, flen), :] = jnp.zeros((flen, half), buf.dtype)

    own_groups = half // width
    row_id = lax.broadcasted_iota(jnp.int32, (flen, flen), 0)
    col_id = lax.broadcasted_iota(jnp.int32, (flen, flen), 1)
    flip = jnp.where(
        (row_id + col_id == flen) | ((row_id == 0) & (col_id == 0)), 1.0, 0.0
    ).astype(jnp.bfloat16)
    for s in range(3):
        turned[s] = jnp.dot(
            filters[s, pl.ds(pl.multiple_of(side * own_groups, own_groups), own_groups), :],
            flip,
            preferred_element_type=jnp.float32,
        )

    def build(h):
        @pl.loop(0, 3)
        def _(s):
            lines = turned[s, pl.ds(pl.multiple_of(h * per_tile, per_tile), per_tile), :]
            for g in range(per_tile):
                table = pltpu.roll(
                    jnp.broadcast_to(lines[g : g + 1], (flen, flen)),
                    0,
                    1,
                    stride=1,
                    stride_axis=0,
                )
                lower = jnp.where(col_id <= row_id, table, 0.0)
                upper = jnp.where(col_id > row_id, table, 0.0)
                where = pl.ds(g * flen, flen)
                toep[s, where, pl.ds(0, flen)] = upper.astype(toep.dtype)
                toep[s, where, pl.ds(flen, flen)] = lower.astype(toep.dtype)

    blocks = span // flen
    lane_group = lax.broadcasted_iota(jnp.int32, (flen, blocks * LANES), 1)
    lane_group = lax.rem(lane_group, LANES) // width

    def fold(values, op):
        result = values[:, :LANES]
        for c in range(1, values.shape[1] // LANES):
            result = op(result, values[:, c * LANES : (c + 1) * LANES])
        return result

    def filter_head(s, h):
        lanes = lanes_of(h)
        window = [buf[s, pl.ds(b * flen, 2 * flen), lanes] for b in range(blocks)]
        product = jnp.dot(
            toep[s], jnp.concatenate(window, axis=1), preferred_element_type=jnp.float32
        )
        result = product[:flen]
        for g in range(1, per_tile):
            result = jnp.where(lane_group == g, product[g * flen : (g + 1) * flen], result)
        result = result.astype(feat.dtype)
        for b in range(blocks):
            feat[s, pl.ds(b * flen, flen), lanes] = result[:, b * LANES : (b + 1) * LANES]

    def attend(query, pieces):
        parts = []
        for key, _, last in pieces:
            block = lax.dot_general(
                query, key, (((1,), (1,)), ((), ())), preferred_element_type=jnp.float32
            )
            if last:
                line = lax.broadcasted_iota(jnp.int32, block.shape, 0)
                spot = lax.broadcasted_iota(jnp.int32, block.shape, 1)
                block = jnp.where(spot <= line, block, -1e30)
            parts.append(block)
        top = functools.reduce(jnp.maximum, [fold(p, jnp.maximum) for p in parts])
        top = jnp.max(top, axis=1, keepdims=True)
        weights = [jnp.exp2((p - top) * factor) for p in parts]
        total = functools.reduce(jnp.add, [fold(w, jnp.add) for w in weights])
        total = jnp.sum(total, axis=1, keepdims=True)
        mixed = [
            jnp.dot(w.astype(jnp.bfloat16), p[1], preferred_element_type=jnp.float32)
            for w, p in zip(weights, pieces)
        ]
        return functools.reduce(jnp.add, mixed), top, total

    def piece(ref, base, h, first, size, last=False):
        where = pl.ds(first, size)
        return (ref[base, where, lanes_of(h)], ref[base + 1, where, lanes_of(h)], last)

    def own_pieces(h, r):
        before = [piece(feat, 1, h, 0, r * rows)] if r else []
        return before + [piece(feat, 1, h, r * rows, rows, True)]

    def query_of(h, r):
        return feat[0, pl.ds(r * rows, rows), lanes_of(h)]

    def finish(h, r, values):
        @pl.when(side == r)
        def _():
            att[:, half_lanes(side, h)] = values

        @pl.when(side != r)
        def _():
            sending[:, lanes_of(h)] = values

    lane_id = lax.broadcasted_iota(jnp.int32, (rows, LANES), 1)

    def serve(d, h, pieces):
        q_copy(d, h).wait_recv()
        results = [
            attend(far_q[d, pl.ds(r * rows, rows), lanes_of(h)], pieces) for r in range(SIDES)
        ]
        for r, (mixed, top, total) in enumerate(results):
            part[d, pl.ds(r * rows, rows), lanes_of(h)] = (mixed / total).astype(part.dtype)
            stat = jnp.where(lane_id == 0, top, total)
            part_stat[d, h, r] = stat.T[:8]
        for r in range(SIDES):
            part_copy(d, h, r).start()
            stat_copy(d, h, r).start()

    def keep(h):
        for r in range(SIDES):
            mixed, top, total = attend(query_of(h, r), own_pieces(h, r))
            own_acc[h, r] = mixed
            own_top[h, r] = jnp.broadcast_to(top, (rows, LANES))
            own_total[h, r] = jnp.broadcast_to(total, (rows, LANES))

    def spread(line):
        return jnp.broadcast_to(line, (LANES, rows)).T

    def merge(h, count):
        for r in range(SIDES):
            for d in range(count):
                part_copy(d, h, r).wait_recv()
                stat_copy(d, h, r).wait_recv()
        for r in range(SIDES):
            where = pl.ds(r * rows, rows)
            tops = [own_top[h, r]] + [spread(in_stat[d, h, r, 0:1, :]) for d in range(count)]
            totals = [own_total[h, r]] + [spread(in_stat[d, h, r, 1:2, :]) for d in range(count)]
            top = functools.reduce(jnp.maximum, tops)
            scales = [jnp.exp2((t - top) * factor) for t in tops]
            total = functools.reduce(jnp.add, [a * b for a, b in zip(scales, totals)])
            mixed = own_acc[h, r] * scales[0]
            for d in range(count):
                values = inbox[d, where, lanes_of(h)].astype(jnp.float32)
                mixed = mixed + values * (scales[d + 1] * totals[d + 1])
            finish(h, r, (mixed / total).astype(jnp.bfloat16))
        back_copy(h, side).start()

    @pl.loop(0, heads)
    def _(h):
        build(h)

        @pl.when(h == 0)
        def _():
            own_copy().wait()

        @pl.when(layer > 0)
        def _():
            halo_copy(h, 0).wait_recv()

        @pl.loop(0, 3)
        def _(j):
            s = stream_at(j)
            side_copy(s, h, side).wait_recv()
            filter_head(s, h)

            @pl.when((layer == 0) & (j == 1))
            def _():
                kv_copy(h).start()

            @pl.when((layer == LAYERS - 1) & (j == 0))
            def _():
                q_copy(1, h).start()

            @pl.when((layer > HUB) & (j == 0))
            def _():
                q_copy(0, h).start()

        @pl.when(layer == 0)
        def _():
            for r in range(SIDES):
                mixed, _, total = attend(query_of(h, r), own_pieces(h, r))
                finish(h, r, (mixed / total).astype(jnp.bfloat16))
            back_copy(h, side).start()

        @pl.when(layer == HUB)
        def _():
            kv_copy(h).wait_recv()
            far = piece(far_kv, 0, h, 0, span)
            for r in range(SIDES):
                mixed, _, total = attend(query_of(h, r), [far] + own_pieces(h, r))
                finish(h, r, (mixed / total).astype(jnp.bfloat16))
            back_copy(h, side).start()

            @pl.loop(0, LAYERS - 1 - HUB)
            def _(d):
                serve(d, h, [piece(far_kv, 0, h, 0, span), piece(feat, 1, h, 0, span)])

        @pl.when(layer > HUB)
        def _():
            keep(h)

        @pl.when((layer > HUB) & (layer < LAYERS - 1))
        def _():
            serve(0, h, [piece(feat, 1, h, 0, span)])

    @pl.when(layer == LAYERS - 2)
    def _():
        @pl.loop(0, heads)
        def _(h):
            merge(h, 1)

    @pl.when(layer == LAYERS - 1)
    def _():
        @pl.loop(0, heads)
        def _(h):
            merge(h, 2)

    @pl.loop(0, heads)
    def _(h):
        back_copy(h, side).wait_recv()

    row_blocks = rows // flen

    @pl.loop(0, row_blocks)
    def _(b):
        where = pl.ds(pl.multiple_of(b * flen, flen), flen)
        wide = att[where, :].astype(jnp.float32)
        squares = fold(wide * wide, jnp.add).T
        squares = squares.reshape(LANES // 8, 8, flen)
        sums[0, :, where] = jnp.sum(squares, axis=0)

    def sum_copy(k):
        return remote(
            sums.at[0],
            sums.at[k],
            sum_send.at[k],
            sum_recv.at[k],
            {"grp": lax.rem(my_grp + k, n_grp)},
        )

    for k in range(1, n_grp):
        sum_copy(k).start()
    for k in range(1, n_grp):
        sum_copy(k).wait()

    @pl.loop(0, row_blocks)
    def _(b):
        where = pl.ds(pl.multiple_of(b * flen, flen), flen)
        power = sums[0, :, where]
        for k in range(1, n_grp):
            power = power + sums[k, :, where]
        power = jnp.sum(power, axis=0, keepdims=True) / (chans * n_grp)
        power = jnp.broadcast_to(lax.rsqrt(power + 1e-06), (LANES, flen)).T
        wide = att[where, :].astype(jnp.float32)
        for c in range(chans // LANES):
            lanes = slice(c * LANES, (c + 1) * LANES)
            out[where, lanes] = (wide[:, lanes] * gain[:, lanes] * power).astype(out.dtype)

    @pl.loop(0, heads)
    def _(h):
        for s in range(3):
            side_copy(s, h, side).wait_send()
        back_copy(h, side).wait_send()

        @pl.when((side == SIDES - 1) & (layer < LAYERS - 1))
        def _():
            for y in range(SIDES):
                halo_copy(h, y).wait_send()

        @pl.when(layer == 0)
        def _():
            kv_copy(h).wait_send()

        @pl.when(layer > HUB)
        def _():
            q_copy(0, h).wait_send()

        @pl.when(layer == LAYERS - 1)
        def _():
            q_copy(1, h).wait_send()

        @pl.when((layer >= HUB) & (layer < LAYERS - 1))
        def _():
            for r in range(SIDES):
                part_copy(0, h, r).wait_send()
                stat_copy(0, h, r).wait_send()

        @pl.when(layer == HUB)
        def _():
            for r in range(SIDES):
                part_copy(1, h, r).wait_send()
                stat_copy(1, h, r).wait_send()


def layered(streams, filters, gain):
    n, n_grp = lax.axis_size("ctx"), lax.axis_size("grp")
    _, rows, chans = streams.shape
    _, groups, flen = filters.shape
    half = chans // SIDES
    heads = half // HD
    span = rows * SIDES
    per_tile = LANES * groups // chans
    vmem = pl.BlockSpec(memory_space=pltpu.VMEM)
    dma = pltpu.SemaphoreType.DMA
    low = jnp.bfloat16
    far = LAYERS - 1 - HUB
    return pl.pallas_call(
        functools.partial(layered_kernel, n, n_grp),
        out_shape=jax.ShapeDtypeStruct((rows, chans), low),
        in_specs=[pl.BlockSpec(memory_space=pl.ANY), vmem, vmem],
        out_specs=vmem,
        scratch_shapes=[
            pltpu.VMEM((3, flen + span, half), low),
            pltpu.VMEM((3, groups // SIDES, flen), jnp.float32),
            pltpu.VMEM((3, per_tile * flen, 2 * flen), low),
            pltpu.VMEM((3, span, half), low),
            pltpu.VMEM((2, span, half), low),
            pltpu.VMEM((far, span, half), low),
            pltpu.VMEM((far, span, half), low),
            pltpu.VMEM((far, heads, SIDES, 8, rows), jnp.float32),
            pltpu.VMEM((far, span, half), low),
            pltpu.VMEM((far, heads, SIDES, 8, rows), jnp.float32),
            pltpu.VMEM((heads, SIDES, rows, HD), jnp.float32),
            pltpu.VMEM((heads, SIDES, rows, LANES), jnp.float32),
            pltpu.VMEM((heads, SIDES, rows, LANES), jnp.float32),
            pltpu.VMEM((rows, half), low),
            pltpu.VMEM((rows, chans), low),
            pltpu.VMEM((n_grp, 8, rows), jnp.float32),
            dma((1,)),
            dma((3, heads)),
            dma((3, heads)),
            dma((SIDES, heads)),
            dma((heads,)),
            dma((heads,)),
            dma((heads,)),
            dma((far, heads)),
            dma((far, heads)),
            dma((far, heads, SIDES)),
            dma((far, heads, SIDES)),
            dma((far, heads, SIDES)),
            dma((far, heads, SIDES)),
            dma((heads,)),
            dma((heads,)),
            dma((n_grp,)),
            dma((n_grp,)),
        ],
        compiler_params=pltpu.CompilerParams(
            collective_id=0, has_side_effects=True, vmem_limit_bytes=56 * 2**20
        ),
        name="layered",
    )(streams, filters, gain.reshape(1, chans))


def passed_along(block, axis, distance):
    devices = range(lax.axis_size(axis))
    route = [(i - distance, i) for i in devices if i - distance in devices]
    return lax.ppermute(block, axis, route)


def filter_all(streams, filters):
    tok_rows = streams.shape[1]
    chan_count = streams.shape[2]
    filt_len = filters.shape[2]
    group_count = filters.shape[1]
    group_width = chan_count // group_count
    tail = streams[:, tok_rows - filt_len :, :]
    before = passed_along(tail, "ctx", 1)
    padded = jnp.concatenate([before, streams], axis=1)
    block_count = tok_rows // filt_len
    blocks = padded.reshape(3, block_count + 1, filt_len, group_count, group_width)
    zeros = jnp.zeros_like(filters)
    line = jnp.concatenate([zeros[..., :1], filters[..., ::-1], zeros], axis=2)
    table = jnp.broadcast_to(line[:, :, None, :], line.shape[:2] + (filt_len, line.shape[2]))
    table = table.reshape(3, group_count, -1)[..., : 2 * filt_len * filt_len]
    table = table.reshape(3, group_count, filt_len, 2 * filt_len)
    upper, lower = table[..., :filt_len], table[..., filt_len:]
    result = jnp.einsum(
        "agts,absgc->abtgc", lower, blocks[:, 1:], preferred_element_type=jnp.float32
    )
    result = result + jnp.einsum(
        "agts,absgc->abtgc", upper, blocks[:, :-1], preferred_element_type=jnp.float32
    )
    return result.reshape(3, tok_rows, chan_count).astype(jnp.bfloat16)


def attend(queries, positions, keyed, valued):
    tok_rows, chan_count = queries.shape
    head_count = chan_count // HD
    scale = HD ** (-0.5)
    query_heads = queries.reshape(tok_rows, head_count, HD)
    query_last = jnp.max(positions)
    start_state = (
        jnp.full((head_count, tok_rows), -1e30, jnp.float32),
        jnp.zeros((head_count, tok_rows), jnp.float32),
        jnp.zeros((tok_rows, head_count, HD), jnp.float32),
    )
    key_piece = lax.all_gather(keyed, "ctx", axis=0, tiled=True)
    value_piece = lax.all_gather(valued, "ctx", axis=0, tiled=True)
    piece_len = key_piece.shape[0]
    block_len = math.gcd(piece_len, 512)

    def step_block(step_idx, state):
        offset = step_idx * block_len
        key_block = lax.dynamic_slice_in_dim(key_piece, offset, block_len, 0).reshape(
            block_len, head_count, HD
        )
        value_block = lax.dynamic_slice_in_dim(value_piece, offset, block_len, 0).reshape(
            block_len, head_count, HD
        )
        key_pos = offset + jnp.arange(block_len, dtype=jnp.int32)

        def update_block(inner):
            running, totals, accum = inner
            scores = (
                jnp.einsum(
                    "shd,khd->hsk", query_heads, key_block, preferred_element_type=jnp.float32
                )
                * scale
            )
            causal = key_pos[None, None, :] <= positions[None, :, None]
            newtop = jnp.maximum(running, jnp.max(jnp.where(causal, scores, -1e30), axis=2))
            weights = jnp.where(causal, jnp.exp(scores - newtop[:, :, None]), 0.0)
            factor = jnp.exp(running - newtop)
            totals = totals * factor + jnp.sum(weights, axis=2)
            accum = accum * factor.T[:, :, None] + jnp.einsum(
                "hsk,khd->shd",
                weights.astype(jnp.bfloat16),
                value_block,
                preferred_element_type=jnp.float32,
            )
            return (newtop, totals, accum)

        return lax.cond(offset > query_last, lambda inner: inner, update_block, state)

    running, totals, accum = lax.fori_loop(0, piece_len // block_len, step_block, start_state)
    return (accum / totals.T[:, :, None]).reshape(tok_rows, chan_count).astype(jnp.bfloat16)


def local(streams, filters, gain):
    features = filter_all(streams, filters)
    tok_rows = streams.shape[1]
    my_index = lax.axis_index("ctx")
    queries = features[0]
    positions = my_index * tok_rows + jnp.arange(tok_rows, dtype=jnp.int32)
    attended = attend(queries, positions, features[1], features[2])
    wide = attended.astype(jnp.float32)
    power = lax.psum(jnp.sum(wide * wide, axis=1), "grp") / (streams.shape[2] * lax.axis_size("grp"))
    return (wide * gain[None, :] * lax.rsqrt(power + 1e-06)[:, None]).astype(jnp.bfloat16)


def chosen(streams, filters, gain):
    n = lax.axis_size("ctx")
    _, rows, chans = streams.shape
    _, groups, flen = filters.shape
    whole_heads = chans % (SIDES * HD) == 0
    fits = flen == LANES and rows % flen == 0 and LANES % (chans // groups) == 0
    if n == SIDES * LAYERS and whole_heads and fits:
        return layered(streams, filters, gain)
    return local(streams, filters, gain)


def solution(mesh):
    placed = (P(None, "ctx", "grp"), P(None, "grp", None), P("grp"))
    return jax.shard_map(
        chosen, mesh=mesh, in_specs=placed, out_specs=P("ctx", "grp"), check_vma=False
    )
```

```python
import functools
import math

import jax
import jax.numpy as jnp
import numpy as np
from jax import lax
from jax.experimental import pallas as pl
from jax.experimental.pallas import tpu as pltpu
from jax.sharding import PartitionSpec as P

HD = 128
LANES = 128
MESH = pl.DeviceIdType.MESH
SIDES = 2
LAYERS = 4
HUB = 1


def layered_kernel(
    n,
    n_grp,
    streams,
    filters,
    gain,
    out,
    buf,
    turned,
    toep,
    feat,
    far_kv,
    far_q,
    part,
    part_stat,
    inbox,
    in_stat,
    own_acc,
    own_top,
    own_total,
    sending,
    att,
    sums,
    local_sem,
    side_send,
    side_recv,
    halo_send,
    halo_recv,
    kv_send,
    kv_recv,
    q_send,
    q_recv,
    part_send,
    part_recv,
    stat_send,
    stat_recv,
    back_send,
    back_recv,
    sum_send,
    sum_recv,
):
    me = lax.axis_index("ctx")
    my_grp = lax.axis_index("grp")
    layer = me // SIDES
    side = lax.rem(me, SIDES)
    other = 1 - side
    rows = streams.shape[1]
    chans = streams.shape[2]
    groups = filters.shape[1]
    flen = filters.shape[2]
    half = chans // SIDES
    heads = half // HD
    span = rows * SIDES
    width = chans // groups
    per_tile = LANES // width
    factor = HD ** (-0.5) * math.log2(math.e)

    def place(z, y):
        return {"ctx": z * SIDES + y}

    def lanes_of(h):
        return pl.ds(pl.multiple_of(h * HD, HD), HD)

    def half_lanes(y, h):
        return pl.ds(pl.multiple_of(y * half + h * HD, HD), HD)

    def remote(src, dst, send, recv, device):
        return pltpu.make_async_remote_copy(
            src_ref=src,
            dst_ref=dst,
            send_sem=send,
            recv_sem=recv,
            device_id=device,
            device_id_type=MESH,
        )

    def own_copy():
        start = pl.multiple_of(flen + side * rows, flen)
        return pltpu.make_async_copy(
            streams.at[:, :, pl.ds(pl.multiple_of(side * half, HD), half)],
            buf.at[:, pl.ds(start, rows), :],
            local_sem.at[0],
        )

    spans = ((rows - flen, flen), (0, rows - flen))

    def side_copy(s, h, p):
        first, size = spans[p]
        start = pl.multiple_of(flen + side * rows + first, flen)
        return remote(
            streams.at[s, pl.ds(first, size), half_lanes(other, h)],
            buf.at[s, pl.ds(start, size), lanes_of(h)],
            side_send.at[s, h, p],
            side_recv.at[s, h, p],
            place(layer, other),
        )

    def halo_copy(s, h):
        return remote(
            buf.at[s, pl.ds(span, flen), lanes_of(h)],
            buf.at[s, pl.ds(0, flen), lanes_of(h)],
            halo_send.at[s, h],
            halo_recv.at[s, h],
            place(lax.rem(layer + 1, LAYERS), side),
        )

    def own_halo_copy(s, h):
        return remote(
            streams.at[s, pl.ds(rows - flen, flen), half_lanes(side, h)],
            buf.at[s, pl.ds(0, flen), lanes_of(h)],
            halo_send.at[s, h],
            halo_recv.at[s, h],
            place(lax.rem(layer + 1, LAYERS), side),
        )

    def kv_copy(j, h):
        return remote(
            feat.at[1 + j, :, lanes_of(h)],
            far_kv.at[j, :, lanes_of(h)],
            kv_send.at[j, h],
            kv_recv.at[j, h],
            place(HUB, side),
        )

    def q_copy(d, h):
        return remote(
            feat.at[0, :, lanes_of(h)],
            far_q.at[d, :, lanes_of(h)],
            q_send.at[d, h],
            q_recv.at[d, h],
            place(lax.rem(layer + LAYERS - d - 1, LAYERS), side),
        )

    def part_copy(d, h, r):
        where = pl.ds(r * rows, rows)
        return remote(
            part.at[d, where, lanes_of(h)],
            inbox.at[d, where, lanes_of(h)],
            part_send.at[d, h, r],
            part_recv.at[d, h, r],
            place(lax.rem(layer + d + 1, LAYERS), side),
        )

    def stat_copy(d, h, r):
        return remote(
            part_stat.at[d, h, r],
            in_stat.at[d, h, r],
            stat_send.at[d, h, r],
            stat_recv.at[d, h, r],
            place(lax.rem(layer + d + 1, LAYERS), side),
        )

    def back_copy(h, y):
        return remote(
            sending.at[:, lanes_of(h)],
            att.at[:, half_lanes(y, h)],
            back_send.at[h],
            back_recv.at[h],
            place(layer, other),
        )

    barrier = pltpu.get_barrier_semaphore()
    for k in range(1, n):
        pl.semaphore_signal(
            barrier, inc=1, device_id={"ctx": lax.rem(me + k, n)}, device_id_type=MESH
        )
    for k in range(1, n_grp):
        pl.semaphore_signal(
            barrier, inc=1, device_id={"grp": lax.rem(my_grp + k, n_grp)}, device_id_type=MESH
        )
    own_copy().start()
    pl.semaphore_wait(barrier, n - 1 + n_grp - 1)

    last = layer == LAYERS - 1
    sends_own_halo = (side == SIDES - 1) & jnp.logical_not(last)
    passes_halo = (side < SIDES - 1) & jnp.logical_not(last)

    def send_side(s, h):
        for p in range(2):
            side_copy(s, h, p).start()

    @pl.when(layer == 0)
    def _():
        @pl.loop(0, heads)
        def _(h):
            send_side(1, h)
            send_side(2, h)

            @pl.when(h == 0)
            def _():
                for k in range(heads):
                    side_copy(0, k, 0).start()

        @pl.loop(0, heads)
        def _(h):
            side_copy(0, h, 1).start()

    @pl.when(layer == HUB)
    def _():
        @pl.loop(0, heads)
        def _(h):
            side_copy(0, h, 0).start()

        @pl.loop(0, heads)
        def _(h):
            send_side(1, h)
            send_side(2, h)
            side_copy(0, h, 1).start()

    @pl.when(layer > HUB)
    def _():
        @pl.loop(0, heads)
        def _(h):
            send_side(0, h)

        @pl.loop(0, heads)
        def _(h):
            send_side(1, h)
            send_side(2, h)

    @pl.when(sends_own_halo & (layer == 0))
    def _():
        @pl.loop(0, heads)
        def _(h):
            own_halo_copy(1, h).start()
            own_halo_copy(2, h).start()
            own_halo_copy(0, h).start()

    @pl.when(sends_own_halo & (layer > 0))
    def _():
        @pl.loop(0, heads)
        def _(h):
            own_halo_copy(0, h).start()

        @pl.loop(0, heads)
        def _(h):
            own_halo_copy(1, h).start()
            own_halo_copy(2, h).start()

    @pl.when(layer == 0)
    def _():
        for s in range(3):
            buf[s, pl.ds(0, flen), :] = jnp.zeros((flen, half), buf.dtype)

    own_groups = half // width
    row_id = lax.broadcasted_iota(jnp.int32, (flen, flen), 0)
    col_id = lax.broadcasted_iota(jnp.int32, (flen, flen), 1)
    flip = jnp.where(
        (row_id + col_id == flen) | ((row_id == 0) & (col_id == 0)), 1.0, 0.0
    ).astype(jnp.bfloat16)
    for s in range(3):
        turned[s] = jnp.dot(
            filters[s, pl.ds(pl.multiple_of(side * own_groups, own_groups), own_groups), :],
            flip,
            preferred_element_type=jnp.float32,
        )

    def build(s, h):
        lines = turned[s, pl.ds(pl.multiple_of(h * per_tile, per_tile), per_tile), :]
        for g in range(per_tile):
            table = pltpu.roll(
                jnp.broadcast_to(lines[g : g + 1], (flen, flen)), 0, 1, stride=1, stride_axis=0
            )
            lower = jnp.where(col_id <= row_id, table, 0.0)
            upper = jnp.where(col_id > row_id, table, 0.0)
            where = pl.ds(g * flen, flen)
            toep[where, pl.ds(0, flen)] = upper.astype(toep.dtype)
            toep[where, pl.ds(flen, flen)] = lower.astype(toep.dtype)

    blocks = span // flen
    lane_group = lax.broadcasted_iota(jnp.int32, (flen, blocks * LANES), 1)
    lane_group = lax.rem(lane_group, LANES) // width

    def fold(values, op):
        result = values[:, :LANES]
        for c in range(1, values.shape[1] // LANES):
            result = op(result, values[:, c * LANES : (c + 1) * LANES])
        return result

    def filter_head(s, h):
        lanes = lanes_of(h)
        window = [buf[s, pl.ds(b * flen, 2 * flen), lanes] for b in range(blocks)]
        product = jnp.dot(
            toep[...], jnp.concatenate(window, axis=1), preferred_element_type=jnp.float32
        )
        result = product[:flen]
        for g in range(1, per_tile):
            result = jnp.where(lane_group == g, product[g * flen : (g + 1) * flen], result)
        result = result.astype(feat.dtype)
        for b in range(blocks):
            feat[s, pl.ds(b * flen, flen), lanes] = result[:, b * LANES : (b + 1) * LANES]

    def take_tail(s, h):
        side_copy(s, h, 0).wait_recv()

        @pl.when(passes_halo)
        def _():
            halo_copy(s, h).start()

    def step(s, h, tail=True):
        build(s, h)
        if tail:
            take_tail(s, h)
        side_copy(s, h, 1).wait_recv()

        @pl.when(layer > 0)
        def _():
            halo_copy(s, h).wait_recv()

        filter_head(s, h)

    def attend(query, pieces):
        parts = []
        for key, _, last in pieces:
            block = lax.dot_general(
                query, key, (((1,), (1,)), ((), ())), preferred_element_type=jnp.float32
            )
            if last:
                line = lax.broadcasted_iota(jnp.int32, block.shape, 0)
                spot = lax.broadcasted_iota(jnp.int32, block.shape, 1)
                block = jnp.where(spot <= line, block, -1e30)
            parts.append(block)
        top = functools.reduce(jnp.maximum, [fold(p, jnp.maximum) for p in parts])
        top = jnp.max(top, axis=1, keepdims=True)
        weights = [jnp.exp2((p - top) * factor) for p in parts]
        total = functools.reduce(jnp.add, [fold(w, jnp.add) for w in weights])
        total = jnp.sum(total, axis=1, keepdims=True)
        mixed = [
            jnp.dot(w.astype(jnp.bfloat16), p[1], preferred_element_type=jnp.float32)
            for w, p in zip(weights, pieces)
        ]
        return functools.reduce(jnp.add, mixed), top, total

    def piece(ref, base, h, first, size, last=False):
        where = pl.ds(first, size)
        return (ref[base, where, lanes_of(h)], ref[base + 1, where, lanes_of(h)], last)

    def own_pieces(h, r):
        before = [piece(feat, 1, h, 0, r * rows)] if r else []
        return before + [piece(feat, 1, h, r * rows, rows, True)]

    def query_of(h, r):
        return feat[0, pl.ds(r * rows, rows), lanes_of(h)]

    def finish(h, r, values):
        @pl.when(side == r)
        def _():
            att[:, half_lanes(side, h)] = values

        @pl.when(side != r)
        def _():
            sending[:, lanes_of(h)] = values

    lane_id = lax.broadcasted_iota(jnp.int32, (rows, LANES), 1)

    def serve(d, h, pieces):
        q_copy(d, h).wait_recv()
        results = [
            attend(far_q[d, pl.ds(r * rows, rows), lanes_of(h)], pieces) for r in range(SIDES)
        ]
        for r, (mixed, top, total) in enumerate(results):
            part[d, pl.ds(r * rows, rows), lanes_of(h)] = (mixed / total).astype(part.dtype)
            stat = jnp.where(lane_id == 0, top, total)
            part_stat[d, h, r] = stat.T[:8]
        for r in range(SIDES):
            part_copy(d, h, r).start()
            stat_copy(d, h, r).start()

    def keep(h):
        for r in range(SIDES):
            mixed, top, total = attend(query_of(h, r), own_pieces(h, r))
            own_acc[h, r] = mixed
            own_top[h, r] = jnp.broadcast_to(top, (rows, LANES))
            own_total[h, r] = jnp.broadcast_to(total, (rows, LANES))

    def spread(line):
        return jnp.broadcast_to(line, (LANES, rows)).T

    def merge(h, count):
        for r in range(SIDES):
            for d in range(count):
                part_copy(d, h, r).wait_recv()
                stat_copy(d, h, r).wait_recv()
        for r in range(SIDES):
            where = pl.ds(r * rows, rows)
            tops = [own_top[h, r]] + [spread(in_stat[d, h, r, 0:1, :]) for d in range(count)]
            totals = [own_total[h, r]] + [spread(in_stat[d, h, r, 1:2, :]) for d in range(count)]
            top = functools.reduce(jnp.maximum, tops)
            scales = [jnp.exp2((t - top) * factor) for t in tops]
            total = functools.reduce(jnp.add, [a * b for a, b in zip(scales, totals)])
            mixed = own_acc[h, r] * scales[0]
            for d in range(count):
                values = inbox[d, where, lanes_of(h)].astype(jnp.float32)
                mixed = mixed + values * (scales[d + 1] * totals[d + 1])
            finish(h, r, (mixed / total).astype(jnp.bfloat16))
        back_copy(h, side).start()

    own_copy().wait()

    @pl.when(layer == 0)
    def _():
        @pl.loop(0, heads)
        def _(h):
            @pl.loop(0, 2)
            def _(j):
                step(1 + j, h)
                kv_copy(j, h).start()

            @pl.when(h == 0)
            def _():
                for k in range(heads):
                    take_tail(0, k)

        @pl.loop(0, heads)
        def _(h):
            step(0, h, False)
            for r in range(SIDES):
                mixed, _, total = attend(query_of(h, r), own_pieces(h, r))
                finish(h, r, (mixed / total).astype(jnp.bfloat16))
            back_copy(h, side).start()

    @pl.when(layer == HUB)
    def _():
        @pl.loop(0, heads)
        def _(h):
            take_tail(0, h)

        for j in range(2):
            take_tail(1 + j, 0)

        @pl.loop(0, heads)
        def _(h):
            @pl.loop(0, 2)
            def _(j):
                step(1 + j, h, False)

            @pl.when(h + 1 < heads)
            def _():
                for j in range(2):
                    take_tail(1 + j, h + 1)

            for j in range(2):
                kv_copy(j, h).wait_recv()

            @pl.loop(0, LAYERS - 1 - HUB)
            def _(d):
                serve(d, h, [piece(far_kv, 0, h, 0, span), piece(feat, 1, h, 0, span)])

            step(0, h, False)
            far = piece(far_kv, 0, h, 0, span)
            for r in range(SIDES):
                mixed, _, total = attend(query_of(h, r), [far] + own_pieces(h, r))
                finish(h, r, (mixed / total).astype(jnp.bfloat16))
            back_copy(h, side).start()

    @pl.when(layer > HUB)
    def _():
        @pl.loop(0, heads)
        def _(h):
            step(0, h)

            @pl.when(last)
            def _():
                q_copy(1, h).start()

            q_copy(0, h).start()

        @pl.loop(0, heads)
        def _(h):
            @pl.loop(0, 2)
            def _(j):
                step(1 + j, h)

            keep(h)

            @pl.when(jnp.logical_not(last))
            def _():
                serve(0, h, [piece(feat, 1, h, 0, span)])

    @pl.when(layer == LAYERS - 2)
    def _():
        @pl.loop(0, heads)
        def _(h):
            merge(h, 1)

    @pl.when(layer == LAYERS - 1)
    def _():
        @pl.loop(0, heads)
        def _(h):
            merge(h, 2)

    @pl.loop(0, heads)
    def _(h):
        back_copy(h, side).wait_recv()

    row_blocks = rows // flen

    @pl.loop(0, row_blocks)
    def _(b):
        where = pl.ds(pl.multiple_of(b * flen, flen), flen)
        wide = att[where, :].astype(jnp.float32)
        squares = fold(wide * wide, jnp.add).T
        squares = squares.reshape(LANES // 8, 8, flen)
        sums[0, :, where] = jnp.sum(squares, axis=0)

    def sum_copy(k):
        return remote(
            sums.at[0],
            sums.at[k],
            sum_send.at[k],
            sum_recv.at[k],
            {"grp": lax.rem(my_grp + k, n_grp)},
        )

    for k in range(1, n_grp):
        sum_copy(k).start()
    for k in range(1, n_grp):
        sum_copy(k).wait()

    @pl.loop(0, row_blocks)
    def _(b):
        where = pl.ds(pl.multiple_of(b * flen, flen), flen)
        power = sums[0, :, where]
        for k in range(1, n_grp):
            power = power + sums[k, :, where]
        power = jnp.sum(power, axis=0, keepdims=True) / (chans * n_grp)
        power = jnp.broadcast_to(lax.rsqrt(power + 1e-06), (LANES, flen)).T
        wide = att[where, :].astype(jnp.float32)
        for c in range(chans // LANES):
            lanes = slice(c * LANES, (c + 1) * LANES)
            out[where, lanes] = (wide[:, lanes] * gain[:, lanes] * power).astype(out.dtype)

    @pl.loop(0, heads)
    def _(h):
        for s in range(3):
            for p in range(2):
                side_copy(s, h, p).wait_send()
        back_copy(h, side).wait_send()

        @pl.when(jnp.logical_not(last))
        def _():
            for s in range(3):
                halo_copy(s, h).wait_send()

        @pl.when(layer == 0)
        def _():
            for j in range(2):
                kv_copy(j, h).wait_send()

        @pl.when(layer > HUB)
        def _():
            q_copy(0, h).wait_send()

        @pl.when(layer == LAYERS - 1)
        def _():
            q_copy(1, h).wait_send()

        @pl.when((layer >= HUB) & (layer < LAYERS - 1))
        def _():
            for r in range(SIDES):
                part_copy(0, h, r).wait_send()
                stat_copy(0, h, r).wait_send()

        @pl.when(layer == HUB)
        def _():
            for r in range(SIDES):
                part_copy(1, h, r).wait_send()
                stat_copy(1, h, r).wait_send()


def layered(streams, filters, gain):
    n, n_grp = lax.axis_size("ctx"), lax.axis_size("grp")
    _, rows, chans = streams.shape
    _, groups, flen = filters.shape
    half = chans // SIDES
    heads = half // HD
    span = rows * SIDES
    per_tile = LANES * groups // chans
    vmem = pl.BlockSpec(memory_space=pltpu.VMEM)
    dma = pltpu.SemaphoreType.DMA
    low = jnp.bfloat16
    far = LAYERS - 1 - HUB
    return pl.pallas_call(
        functools.partial(layered_kernel, n, n_grp),
        out_shape=jax.ShapeDtypeStruct((rows, chans), low),
        in_specs=[pl.BlockSpec(memory_space=pl.ANY), vmem, vmem],
        out_specs=vmem,
        scratch_shapes=[
            pltpu.VMEM((3, flen + span, half), low),
            pltpu.VMEM((3, groups // SIDES, flen), jnp.float32),
            pltpu.VMEM((per_tile * flen, 2 * flen), low),
            pltpu.VMEM((3, span, half), low),
            pltpu.VMEM((2, span, half), low),
            pltpu.VMEM((far, span, half), low),
            pltpu.VMEM((far, span, half), low),
            pltpu.VMEM((far, heads, SIDES, 8, rows), jnp.float32),
            pltpu.VMEM((far, span, half), low),
            pltpu.VMEM((far, heads, SIDES, 8, rows), jnp.float32),
            pltpu.VMEM((heads, SIDES, rows, HD), jnp.float32),
            pltpu.VMEM((heads, SIDES, rows, LANES), jnp.float32),
            pltpu.VMEM((heads, SIDES, rows, LANES), jnp.float32),
            pltpu.VMEM((rows, half), low),
            pltpu.VMEM((rows, chans), low),
            pltpu.VMEM((n_grp, 8, rows), jnp.float32),
            dma((1,)),
            dma((3, heads, 2)),
            dma((3, heads, 2)),
            dma((3, heads)),
            dma((3, heads)),
            dma((2, heads)),
            dma((2, heads)),
            dma((far, heads)),
            dma((far, heads)),
            dma((far, heads, SIDES)),
            dma((far, heads, SIDES)),
            dma((far, heads, SIDES)),
            dma((far, heads, SIDES)),
            dma((heads,)),
            dma((heads,)),
            dma((n_grp,)),
            dma((n_grp,)),
        ],
        compiler_params=pltpu.CompilerParams(
            collective_id=0, has_side_effects=True, vmem_limit_bytes=56 * 2**20
        ),
        name="layered",
    )(streams, filters, gain.reshape(1, chans))


def passed_along(block, axis, distance):
    devices = range(lax.axis_size(axis))
    route = [(i - distance, i) for i in devices if i - distance in devices]
    return lax.ppermute(block, axis, route)


def filter_all(streams, filters):
    tok_rows = streams.shape[1]
    chan_count = streams.shape[2]
    filt_len = filters.shape[2]
    group_count = filters.shape[1]
    group_width = chan_count // group_count
    tail = streams[:, tok_rows - filt_len :, :]
    before = passed_along(tail, "ctx", 1)
    padded = jnp.concatenate([before, streams], axis=1)
    block_count = tok_rows // filt_len
    blocks = padded.reshape(3, block_count + 1, filt_len, group_count, group_width)
    zeros = jnp.zeros_like(filters)
    line = jnp.concatenate([zeros[..., :1], filters[..., ::-1], zeros], axis=2)
    table = jnp.broadcast_to(line[:, :, None, :], line.shape[:2] + (filt_len, line.shape[2]))
    table = table.reshape(3, group_count, -1)[..., : 2 * filt_len * filt_len]
    table = table.reshape(3, group_count, filt_len, 2 * filt_len)
    upper, lower = table[..., :filt_len], table[..., filt_len:]
    result = jnp.einsum(
        "agts,absgc->abtgc", lower, blocks[:, 1:], preferred_element_type=jnp.float32
    )
    result = result + jnp.einsum(
        "agts,absgc->abtgc", upper, blocks[:, :-1], preferred_element_type=jnp.float32
    )
    return result.reshape(3, tok_rows, chan_count).astype(jnp.bfloat16)


def attend(queries, positions, keyed, valued):
    tok_rows, chan_count = queries.shape
    head_count = chan_count // HD
    scale = HD ** (-0.5)
    query_heads = queries.reshape(tok_rows, head_count, HD)
    query_last = jnp.max(positions)
    start_state = (
        jnp.full((head_count, tok_rows), -1e30, jnp.float32),
        jnp.zeros((head_count, tok_rows), jnp.float32),
        jnp.zeros((tok_rows, head_count, HD), jnp.float32),
    )
    key_piece = lax.all_gather(keyed, "ctx", axis=0, tiled=True)
    value_piece = lax.all_gather(valued, "ctx", axis=0, tiled=True)
    piece_len = key_piece.shape[0]
    block_len = math.gcd(piece_len, 512)

    def step_block(step_idx, state):
        offset = step_idx * block_len
        key_block = lax.dynamic_slice_in_dim(key_piece, offset, block_len, 0).reshape(
            block_len, head_count, HD
        )
        value_block = lax.dynamic_slice_in_dim(value_piece, offset, block_len, 0).reshape(
            block_len, head_count, HD
        )
        key_pos = offset + jnp.arange(block_len, dtype=jnp.int32)

        def update_block(inner):
            running, totals, accum = inner
            scores = (
                jnp.einsum(
                    "shd,khd->hsk", query_heads, key_block, preferred_element_type=jnp.float32
                )
                * scale
            )
            causal = key_pos[None, None, :] <= positions[None, :, None]
            newtop = jnp.maximum(running, jnp.max(jnp.where(causal, scores, -1e30), axis=2))
            weights = jnp.where(causal, jnp.exp(scores - newtop[:, :, None]), 0.0)
            factor = jnp.exp(running - newtop)
            totals = totals * factor + jnp.sum(weights, axis=2)
            accum = accum * factor.T[:, :, None] + jnp.einsum(
                "hsk,khd->shd",
                weights.astype(jnp.bfloat16),
                value_block,
                preferred_element_type=jnp.float32,
            )
            return (newtop, totals, accum)

        return lax.cond(offset > query_last, lambda inner: inner, update_block, state)

    running, totals, accum = lax.fori_loop(0, piece_len // block_len, step_block, start_state)
    return (accum / totals.T[:, :, None]).reshape(tok_rows, chan_count).astype(jnp.bfloat16)


def local(streams, filters, gain):
    features = filter_all(streams, filters)
    tok_rows = streams.shape[1]
    my_index = lax.axis_index("ctx")
    queries = features[0]
    positions = my_index * tok_rows + jnp.arange(tok_rows, dtype=jnp.int32)
    attended = attend(queries, positions, features[1], features[2])
    wide = attended.astype(jnp.float32)
    power = lax.psum(jnp.sum(wide * wide, axis=1), "grp") / (streams.shape[2] * lax.axis_size("grp"))
    return (wide * gain[None, :] * lax.rsqrt(power + 1e-06)[:, None]).astype(jnp.bfloat16)


def chosen(streams, filters, gain):
    n = lax.axis_size("ctx")
    _, rows, chans = streams.shape
    _, groups, flen = filters.shape
    whole_heads = chans % (SIDES * HD) == 0
    fits = flen == LANES and rows % flen == 0 and LANES % (chans // groups) == 0
    if n == SIDES * LAYERS and whole_heads and fits:
        return layered(streams, filters, gain)
    return local(streams, filters, gain)


def solution(mesh):
    placed = (P(None, "ctx", "grp"), P(None, "grp", None), P("grp"))
    return jax.shard_map(
        chosen, mesh=mesh, in_specs=placed, out_specs=P("ctx", "grp"), check_vma=False
    )
```

```python
import functools
import math

import jax
import jax.numpy as jnp
import numpy as np
from jax import lax
from jax.experimental import pallas as pl
from jax.experimental.pallas import tpu as pltpu
from jax.sharding import PartitionSpec as P

HD = 128
LANES = 128
MESH = pl.DeviceIdType.MESH
SIDES = 2
LAYERS = 4
HUB = 1


def layered_kernel(
    n,
    n_grp,
    streams,
    filters,
    gain,
    out,
    buf,
    turned,
    toep,
    feat,
    far_kv,
    far_q,
    part,
    part_stat,
    inbox,
    in_stat,
    own_acc,
    own_top,
    own_total,
    sending,
    att,
    sums,
    local_sem,
    side_send,
    side_recv,
    halo_send,
    halo_recv,
    kv_send,
    kv_recv,
    q_send,
    q_recv,
    part_send,
    part_recv,
    stat_send,
    stat_recv,
    back_send,
    back_recv,
    sum_send,
    sum_recv,
):
    me = lax.axis_index("ctx")
    my_grp = lax.axis_index("grp")
    layer = me // SIDES
    side = lax.rem(me, SIDES)
    other = 1 - side
    rows = streams.shape[1]
    chans = streams.shape[2]
    groups = filters.shape[1]
    flen = filters.shape[2]
    half = chans // SIDES
    heads = half // HD
    span = rows * SIDES
    width = chans // groups
    per_tile = LANES // width
    factor = HD ** (-0.5) * math.log2(math.e)

    def place(z, y):
        return {"ctx": z * SIDES + y}

    def lanes_of(h):
        return pl.ds(pl.multiple_of(h * HD, HD), HD)

    def half_lanes(y, h):
        return pl.ds(pl.multiple_of(y * half + h * HD, HD), HD)

    def remote(src, dst, send, recv, device):
        return pltpu.make_async_remote_copy(
            src_ref=src,
            dst_ref=dst,
            send_sem=send,
            recv_sem=recv,
            device_id=device,
            device_id_type=MESH,
        )

    def own_copy():
        start = pl.multiple_of(flen + side * rows, flen)
        return pltpu.make_async_copy(
            streams.at[:, :, pl.ds(pl.multiple_of(side * half, HD), half)],
            buf.at[:, pl.ds(start, rows), :],
            local_sem.at[0],
        )

    spans = ((rows - flen, flen), (0, rows - flen))

    def side_copy(s, h, p):
        first, size = spans[p]
        start = pl.multiple_of(flen + side * rows + first, flen)
        return remote(
            streams.at[s, pl.ds(first, size), half_lanes(other, h)],
            buf.at[s, pl.ds(start, size), lanes_of(h)],
            side_send.at[s, h, p],
            side_recv.at[s, h, p],
            place(layer, other),
        )

    def halo_copy(s, h):
        return remote(
            buf.at[s, pl.ds(span, flen), lanes_of(h)],
            buf.at[s, pl.ds(0, flen), lanes_of(h)],
            halo_send.at[s, h],
            halo_recv.at[s, h],
            place(lax.rem(layer + 1, LAYERS), side),
        )

    def own_halo_copy(s, h):
        return remote(
            streams.at[s, pl.ds(rows - flen, flen), half_lanes(side, h)],
            buf.at[s, pl.ds(0, flen), lanes_of(h)],
            halo_send.at[s, h],
            halo_recv.at[s, h],
            place(lax.rem(layer + 1, LAYERS), side),
        )

    def rows_of(r):
        return pl.ds(pl.multiple_of(r * rows, flen), rows)

    def kv_copy(j, h, r):
        return remote(
            feat.at[1 + j, rows_of(r), lanes_of(h)],
            far_kv.at[j, rows_of(r), lanes_of(h)],
            kv_send.at[j, h, r],
            kv_recv.at[j, h, r],
            place(HUB, side),
        )

    def q_copy(d, h):
        return remote(
            feat.at[0, :, lanes_of(h)],
            far_q.at[d, :, lanes_of(h)],
            q_send.at[d, h],
            q_recv.at[d, h],
            place(lax.rem(layer + LAYERS - d - 1, LAYERS), side),
        )

    def part_copy(d, h, r):
        return remote(
            part.at[d, rows_of(r), lanes_of(h)],
            inbox.at[d, rows_of(r), lanes_of(h)],
            part_send.at[d, h, r],
            part_recv.at[d, h, r],
            place(lax.rem(layer + d + 1, LAYERS), side),
        )

    def stat_copy(d, h, r):
        return remote(
            part_stat.at[d, h, r, pl.ds(0, 2)],
            in_stat.at[d, h, r, pl.ds(0, 2)],
            stat_send.at[d, h, r],
            stat_recv.at[d, h, r],
            place(lax.rem(layer + d + 1, LAYERS), side),
        )

    def back_copy(h, y):
        return remote(
            sending.at[:, lanes_of(h)],
            att.at[:, half_lanes(y, h)],
            back_send.at[h],
            back_recv.at[h],
            place(layer, other),
        )

    barrier = pltpu.get_barrier_semaphore()
    for k in range(1, n):
        pl.semaphore_signal(
            barrier, inc=1, device_id={"ctx": lax.rem(me + k, n)}, device_id_type=MESH
        )
    for k in range(1, n_grp):
        pl.semaphore_signal(
            barrier, inc=1, device_id={"grp": lax.rem(my_grp + k, n_grp)}, device_id_type=MESH
        )
    own_copy().start()
    pl.semaphore_wait(barrier, n - 1 + n_grp - 1)

    last = layer == LAYERS - 1
    sends_own_halo = (side == SIDES - 1) & jnp.logical_not(last)
    passes_halo = (side < SIDES - 1) & jnp.logical_not(last)

    def send_side(s, h):
        for p in range(2):
            side_copy(s, h, p).start()

    @pl.when(layer == 0)
    def _():
        @pl.loop(0, heads)
        def _(h):
            send_side(1, h)
            send_side(2, h)
            side_copy(0, h, 0).start()

        @pl.loop(0, heads)
        def _(h):
            side_copy(0, h, 1).start()

    @pl.when(layer == HUB)
    def _():
        @pl.loop(0, heads)
        def _(h):
            side_copy(0, h, 0).start()

        @pl.loop(0, heads)
        def _(h):
            for s in (1, 2):
                side_copy(s, h, 0).start()

        @pl.loop(0, heads)
        def _(h):
            for s in (1, 2, 0):
                side_copy(s, h, 1).start()

    @pl.when(layer > HUB)
    def _():
        @pl.loop(0, heads)
        def _(h):
            send_side(0, h)

        @pl.loop(0, heads)
        def _(h):
            send_side(1, h)
            send_side(2, h)

    @pl.when(sends_own_halo & (layer == 0))
    def _():
        for s in range(3):
            own_halo_copy(s, 0).start()

    @pl.when(sends_own_halo & (layer > 0))
    def _():
        @pl.loop(0, heads)
        def _(h):
            own_halo_copy(0, h).start()

        @pl.loop(0, heads)
        def _(h):
            own_halo_copy(1, h).start()
            own_halo_copy(2, h).start()

    @pl.when(layer == 0)
    def _():
        for s in range(3):
            buf[s, pl.ds(0, flen), :] = jnp.zeros((flen, half), buf.dtype)

    own_groups = half // width
    row_id = lax.broadcasted_iota(jnp.int32, (flen, flen), 0)
    col_id = lax.broadcasted_iota(jnp.int32, (flen, flen), 1)
    flip = jnp.where(
        (row_id + col_id == flen) | ((row_id == 0) & (col_id == 0)), 1.0, 0.0
    ).astype(jnp.bfloat16)
    for s in range(3):
        turned[s] = jnp.dot(
            filters[s, pl.ds(pl.multiple_of(side * own_groups, own_groups), own_groups), :],
            flip,
            preferred_element_type=jnp.float32,
        )

    def build(s, h):
        lines = turned[s, pl.ds(pl.multiple_of(h * per_tile, per_tile), per_tile), :]
        for g in range(per_tile):
            table = pltpu.roll(
                jnp.broadcast_to(lines[g : g + 1], (flen, flen)), 0, 1, stride=1, stride_axis=0
            )
            lower = jnp.where(col_id <= row_id, table, 0.0)
            upper = jnp.where(col_id > row_id, table, 0.0)
            where = pl.ds(g * flen, flen)
            toep[where, pl.ds(0, flen)] = upper.astype(toep.dtype)
            toep[where, pl.ds(flen, flen)] = lower.astype(toep.dtype)

    blocks = span // flen
    lane_group = lax.broadcasted_iota(jnp.int32, (flen, blocks * LANES), 1)
    lane_group = lax.rem(lane_group, LANES) // width

    def fold(values, op):
        result = values[:, :LANES]
        for c in range(1, values.shape[1] // LANES):
            result = op(result, values[:, c * LANES : (c + 1) * LANES])
        return result

    def filter_rows(s, h, first, count):
        lanes = lanes_of(h)
        starts = [pl.multiple_of(first + b * flen, flen) for b in range(count)]
        window = [buf[s, pl.ds(start, 2 * flen), lanes] for start in starts]
        product = jnp.dot(
            toep[...], jnp.concatenate(window, axis=1), preferred_element_type=jnp.float32
        )
        result = product[:flen]
        group = lane_group[:, : count * LANES]
        for g in range(1, per_tile):
            result = jnp.where(group == g, product[g * flen : (g + 1) * flen], result)
        result = result.astype(feat.dtype)
        for b, start in enumerate(starts):
            feat[s, pl.ds(start, flen), lanes] = result[:, b * LANES : (b + 1) * LANES]

    def take_tail(s, h):
        side_copy(s, h, 0).wait_recv()

        @pl.when(passes_halo)
        def _():
            halo_copy(s, h).start()

    def step(s, h, tail=True):
        build(s, h)
        if tail:
            take_tail(s, h)
        side_copy(s, h, 1).wait_recv()

        @pl.when(layer > 0)
        def _():
            halo_copy(s, h).wait_recv()

        filter_rows(s, h, 0, blocks)

    def attend(query, pieces):
        parts = []
        for key, _, last in pieces:
            block = lax.dot_general(
                query, key, (((1,), (1,)), ((), ())), preferred_element_type=jnp.float32
            )
            if last:
                line = lax.broadcasted_iota(jnp.int32, block.shape, 0)
                spot = lax.broadcasted_iota(jnp.int32, block.shape, 1)
                block = jnp.where(spot <= line, block, -1e30)
            parts.append(block)
        top = functools.reduce(jnp.maximum, [fold(p, jnp.maximum) for p in parts])
        top = jnp.max(top, axis=1, keepdims=True)
        weights = [jnp.exp2((p - top) * factor) for p in parts]
        total = functools.reduce(jnp.add, [fold(w, jnp.add) for w in weights])
        total = jnp.sum(total, axis=1, keepdims=True)
        mixed = [
            jnp.dot(w.astype(jnp.bfloat16), p[1], preferred_element_type=jnp.float32)
            for w, p in zip(weights, pieces)
        ]
        return functools.reduce(jnp.add, mixed), top, total

    def piece(ref, base, h, first, size, last=False):
        where = pl.ds(first, size)
        return (ref[base, where, lanes_of(h)], ref[base + 1, where, lanes_of(h)], last)

    def own_pieces(h, r):
        before = [piece(feat, 1, h, 0, r * rows)] if r else []
        return before + [piece(feat, 1, h, r * rows, rows, True)]

    def query_of(h, r):
        return feat[0, pl.ds(r * rows, rows), lanes_of(h)]

    def finish(h, values):
        for r in range(SIDES):
            @pl.when(side == r)
            def _():
                att[:, half_lanes(side, h)] = values[r]
                sending[:, lanes_of(h)] = values[1 - r]

    lane_id = lax.broadcasted_iota(jnp.int32, (rows, LANES), 1)

    def serve(count, h, pieces):
        for d in range(count):
            q_copy(d, h).wait_recv()

        @pl.loop(0, SIDES)
        def _(i):
            r = lax.rem(other + i, SIDES)
            results = [
                attend(far_q[d, rows_of(r), lanes_of(h)], pieces) for d in range(count)
            ]
            for d, (mixed, top, total) in reversed(list(enumerate(results))):
                part[d, rows_of(r), lanes_of(h)] = (mixed / total).astype(part.dtype)
                part_stat[d, h, r] = jnp.where(lane_id == 0, top, total).T[:8]
                part_copy(d, h, r).start()
                stat_copy(d, h, r).start()

    def keep(h):
        for r in range(SIDES):
            mixed, top, total = attend(query_of(h, r), own_pieces(h, r))
            own_acc[h, r] = mixed
            own_top[h, r] = jnp.broadcast_to(top, (rows, LANES))
            own_total[h, r] = jnp.broadcast_to(total, (rows, LANES))

    def spread(line):
        return jnp.broadcast_to(line, (LANES, rows)).T

    def merge(h, count):
        @pl.loop(0, SIDES)
        def _(i):
            r = lax.rem(other + i, SIDES)
            for d in range(count):
                part_copy(d, h, r).wait_recv()
                stat_copy(d, h, r).wait_recv()
            tops = [own_top[h, r]] + [spread(in_stat[d, h, r, 0:1, :]) for d in range(count)]
            totals = [own_total[h, r]] + [spread(in_stat[d, h, r, 1:2, :]) for d in range(count)]
            top = functools.reduce(jnp.maximum, tops)
            scales = [jnp.exp2((t - top) * factor) for t in tops]
            total = functools.reduce(jnp.add, [a * b for a, b in zip(scales, totals)])
            mixed = own_acc[h, r] * scales[0]
            for d in range(count):
                values = inbox[d, rows_of(r), lanes_of(h)].astype(jnp.float32)
                mixed = mixed + values * (scales[d + 1] * totals[d + 1])
            values = (mixed / total).astype(jnp.bfloat16)

            @pl.when(i == 0)
            def _():
                sending[:, lanes_of(h)] = values
                back_copy(h, side).start()

            @pl.when(i > 0)
            def _():
                att[:, half_lanes(side, h)] = values

    own_copy().wait()

    @pl.when(layer == 0)
    def _():
        @pl.loop(0, heads)
        def _(h):
            @pl.loop(0, 2)
            def _(j):
                build(1 + j, h)

                @pl.loop(0, SIDES)
                def _(i):
                    r = lax.rem(side + i, SIDES)

                    @pl.when(i != side)
                    def _():
                        take_tail(1 + j, h)

                    @pl.when(i > 0)
                    def _():
                        side_copy(1 + j, h, 1).wait_recv()

                    filter_rows(1 + j, h, r * rows, rows // flen)
                    kv_copy(j, h, r).start()

            take_tail(0, h)

            @pl.when((side == SIDES - 1) & (h + 1 < heads))
            def _():
                for s in range(3):
                    own_halo_copy(s, h + 1).start()

        @pl.loop(0, heads)
        def _(h):
            step(0, h, False)
            results = [attend(query_of(h, r), own_pieces(h, r)) for r in range(SIDES)]
            finish(h, [(mixed / total).astype(jnp.bfloat16) for mixed, _, total in results])
            back_copy(h, side).start()

    @pl.when(layer == HUB)
    def _():
        @pl.loop(0, heads)
        def _(h):
            take_tail(0, h)

        @pl.loop(0, heads)
        def _(h):
            for j in range(2):
                take_tail(1 + j, h)

        @pl.loop(0, heads)
        def _(h):
            @pl.loop(0, 2)
            def _(j):
                step(1 + j, h, False)

            for j in range(2):
                for r in range(SIDES):
                    kv_copy(j, h, r).wait_recv()

            serve(
                LAYERS - 1 - HUB, h, [piece(far_kv, 0, h, 0, span), piece(feat, 1, h, 0, span)]
            )

            step(0, h, False)
            far = piece(far_kv, 0, h, 0, span)
            results = [attend(query_of(h, r), [far] + own_pieces(h, r)) for r in range(SIDES)]
            finish(h, [(mixed / total).astype(jnp.bfloat16) for mixed, _, total in results])
            back_copy(h, side).start()

    @pl.when(layer > HUB)
    def _():
        @pl.loop(0, heads)
        def _(h):
            step(0, h)

            @pl.when(last)
            def _():
                q_copy(1, h).start()

            q_copy(0, h).start()

        @pl.loop(0, heads)
        def _(h):
            @pl.loop(0, 2)
            def _(j):
                step(1 + j, h)

            keep(h)

            @pl.when(jnp.logical_not(last))
            def _():
                serve(1, h, [piece(feat, 1, h, 0, span)])

    @pl.when(layer == LAYERS - 2)
    def _():
        @pl.loop(0, heads)
        def _(h):
            merge(h, 1)

    @pl.when(layer == LAYERS - 1)
    def _():
        @pl.loop(0, heads)
        def _(h):
            merge(h, 2)

    @pl.loop(0, heads)
    def _(h):
        back_copy(h, side).wait_recv()

    row_blocks = rows // flen

    @pl.loop(0, row_blocks)
    def _(b):
        where = pl.ds(pl.multiple_of(b * flen, flen), flen)
        wide = att[where, :].astype(jnp.float32)
        squares = fold(wide * wide, jnp.add).T
        squares = squares.reshape(LANES // 8, 8, flen)
        sums[0, :, where] = jnp.sum(squares, axis=0)

    def sum_copy(k):
        return remote(
            sums.at[0],
            sums.at[k],
            sum_send.at[k],
            sum_recv.at[k],
            {"grp": lax.rem(my_grp + k, n_grp)},
        )

    for k in range(1, n_grp):
        sum_copy(k).start()
    for k in range(1, n_grp):
        sum_copy(k).wait()

    @pl.loop(0, row_blocks)
    def _(b):
        where = pl.ds(pl.multiple_of(b * flen, flen), flen)
        power = sums[0, :, where]
        for k in range(1, n_grp):
            power = power + sums[k, :, where]
        power = jnp.sum(power, axis=0, keepdims=True) / (chans * n_grp)
        power = jnp.broadcast_to(lax.rsqrt(power + 1e-06), (LANES, flen)).T
        wide = att[where, :].astype(jnp.float32)
        for c in range(chans // LANES):
            lanes = slice(c * LANES, (c + 1) * LANES)
            out[where, lanes] = (wide[:, lanes] * gain[:, lanes] * power).astype(out.dtype)

    @pl.loop(0, heads)
    def _(h):
        for s in range(3):
            for p in range(2):
                side_copy(s, h, p).wait_send()
        back_copy(h, side).wait_send()

        @pl.when(jnp.logical_not(last))
        def _():
            for s in range(3):
                halo_copy(s, h).wait_send()

        @pl.when(layer == 0)
        def _():
            for j in range(2):
                for r in range(SIDES):
                    kv_copy(j, h, r).wait_send()

        @pl.when(layer > HUB)
        def _():
            q_copy(0, h).wait_send()

        @pl.when(layer == LAYERS - 1)
        def _():
            q_copy(1, h).wait_send()

        @pl.when((layer >= HUB) & (layer < LAYERS - 1))
        def _():
            for r in range(SIDES):
                part_copy(0, h, r).wait_send()
                stat_copy(0, h, r).wait_send()

        @pl.when(layer == HUB)
        def _():
            for r in range(SIDES):
                part_copy(1, h, r).wait_send()
                stat_copy(1, h, r).wait_send()


def layered(streams, filters, gain):
    n, n_grp = lax.axis_size("ctx"), lax.axis_size("grp")
    _, rows, chans = streams.shape
    _, groups, flen = filters.shape
    half = chans // SIDES
    heads = half // HD
    span = rows * SIDES
    per_tile = LANES * groups // chans
    vmem = pl.BlockSpec(memory_space=pltpu.VMEM)
    dma = pltpu.SemaphoreType.DMA
    low = jnp.bfloat16
    far = LAYERS - 1 - HUB
    return pl.pallas_call(
        functools.partial(layered_kernel, n, n_grp),
        out_shape=jax.ShapeDtypeStruct((rows, chans), low),
        in_specs=[pl.BlockSpec(memory_space=pl.ANY), vmem, vmem],
        out_specs=vmem,
        scratch_shapes=[
            pltpu.VMEM((3, flen + span, half), low),
            pltpu.VMEM((3, groups // SIDES, flen), jnp.float32),
            pltpu.VMEM((per_tile * flen, 2 * flen), low),
            pltpu.VMEM((3, span, half), low),
            pltpu.VMEM((2, span, half), low),
            pltpu.VMEM((far, span, half), low),
            pltpu.VMEM((far, span, half), low),
            pltpu.VMEM((far, heads, SIDES, 8, rows), jnp.float32),
            pltpu.VMEM((far, span, half), low),
            pltpu.VMEM((far, heads, SIDES, 8, rows), jnp.float32),
            pltpu.VMEM((heads, SIDES, rows, HD), jnp.float32),
            pltpu.VMEM((heads, SIDES, rows, LANES), jnp.float32),
            pltpu.VMEM((heads, SIDES, rows, LANES), jnp.float32),
            pltpu.VMEM((rows, half), low),
            pltpu.VMEM((rows, chans), low),
            pltpu.VMEM((n_grp, 8, rows), jnp.float32),
            dma((1,)),
            dma((3, heads, 2)),
            dma((3, heads, 2)),
            dma((3, heads)),
            dma((3, heads)),
            dma((2, heads, SIDES)),
            dma((2, heads, SIDES)),
            dma((far, heads)),
            dma((far, heads)),
            dma((far, heads, SIDES)),
            dma((far, heads, SIDES)),
            dma((far, heads, SIDES)),
            dma((far, heads, SIDES)),
            dma((heads,)),
            dma((heads,)),
            dma((n_grp,)),
            dma((n_grp,)),
        ],
        compiler_params=pltpu.CompilerParams(
            collective_id=0, has_side_effects=True, vmem_limit_bytes=56 * 2**20
        ),
        name="layered",
    )(streams, filters, gain.reshape(1, chans))


def passed_along(block, axis, distance):
    devices = range(lax.axis_size(axis))
    route = [(i - distance, i) for i in devices if i - distance in devices]
    return lax.ppermute(block, axis, route)


def filter_all(streams, filters):
    tok_rows = streams.shape[1]
    chan_count = streams.shape[2]
    filt_len = filters.shape[2]
    group_count = filters.shape[1]
    group_width = chan_count // group_count
    tail = streams[:, tok_rows - filt_len :, :]
    before = passed_along(tail, "ctx", 1)
    padded = jnp.concatenate([before, streams], axis=1)
    block_count = tok_rows // filt_len
    blocks = padded.reshape(3, block_count + 1, filt_len, group_count, group_width)
    zeros = jnp.zeros_like(filters)
    line = jnp.concatenate([zeros[..., :1], filters[..., ::-1], zeros], axis=2)
    table = jnp.broadcast_to(line[:, :, None, :], line.shape[:2] + (filt_len, line.shape[2]))
    table = table.reshape(3, group_count, -1)[..., : 2 * filt_len * filt_len]
    table = table.reshape(3, group_count, filt_len, 2 * filt_len)
    upper, lower = table[..., :filt_len], table[..., filt_len:]
    result = jnp.einsum(
        "agts,absgc->abtgc", lower, blocks[:, 1:], preferred_element_type=jnp.float32
    )
    result = result + jnp.einsum(
        "agts,absgc->abtgc", upper, blocks[:, :-1], preferred_element_type=jnp.float32
    )
    return result.reshape(3, tok_rows, chan_count).astype(jnp.bfloat16)


def attend(queries, positions, keyed, valued):
    tok_rows, chan_count = queries.shape
    head_count = chan_count // HD
    scale = HD ** (-0.5)
    query_heads = queries.reshape(tok_rows, head_count, HD)
    query_last = jnp.max(positions)
    start_state = (
        jnp.full((head_count, tok_rows), -1e30, jnp.float32),
        jnp.zeros((head_count, tok_rows), jnp.float32),
        jnp.zeros((tok_rows, head_count, HD), jnp.float32),
    )
    key_piece = lax.all_gather(keyed, "ctx", axis=0, tiled=True)
    value_piece = lax.all_gather(valued, "ctx", axis=0, tiled=True)
    piece_len = key_piece.shape[0]
    block_len = math.gcd(piece_len, 512)

    def step_block(step_idx, state):
        offset = step_idx * block_len
        key_block = lax.dynamic_slice_in_dim(key_piece, offset, block_len, 0).reshape(
            block_len, head_count, HD
        )
        value_block = lax.dynamic_slice_in_dim(value_piece, offset, block_len, 0).reshape(
            block_len, head_count, HD
        )
        key_pos = offset + jnp.arange(block_len, dtype=jnp.int32)

        def update_block(inner):
            running, totals, accum = inner
            scores = (
                jnp.einsum(
                    "shd,khd->hsk", query_heads, key_block, preferred_element_type=jnp.float32
                )
                * scale
            )
            causal = key_pos[None, None, :] <= positions[None, :, None]
            newtop = jnp.maximum(running, jnp.max(jnp.where(causal, scores, -1e30), axis=2))
            weights = jnp.where(causal, jnp.exp(scores - newtop[:, :, None]), 0.0)
            factor = jnp.exp(running - newtop)
            totals = totals * factor + jnp.sum(weights, axis=2)
            accum = accum * factor.T[:, :, None] + jnp.einsum(
                "hsk,khd->shd",
                weights.astype(jnp.bfloat16),
                value_block,
                preferred_element_type=jnp.float32,
            )
            return (newtop, totals, accum)

        return lax.cond(offset > query_last, lambda inner: inner, update_block, state)

    running, totals, accum = lax.fori_loop(0, piece_len // block_len, step_block, start_state)
    return (accum / totals.T[:, :, None]).reshape(tok_rows, chan_count).astype(jnp.bfloat16)


def local(streams, filters, gain):
    features = filter_all(streams, filters)
    tok_rows = streams.shape[1]
    my_index = lax.axis_index("ctx")
    queries = features[0]
    positions = my_index * tok_rows + jnp.arange(tok_rows, dtype=jnp.int32)
    attended = attend(queries, positions, features[1], features[2])
    wide = attended.astype(jnp.float32)
    power = lax.psum(jnp.sum(wide * wide, axis=1), "grp") / (streams.shape[2] * lax.axis_size("grp"))
    return (wide * gain[None, :] * lax.rsqrt(power + 1e-06)[:, None]).astype(jnp.bfloat16)


def chosen(streams, filters, gain):
    n = lax.axis_size("ctx")
    _, rows, chans = streams.shape
    _, groups, flen = filters.shape
    whole_heads = chans % (SIDES * HD) == 0
    fits = flen == LANES and rows % flen == 0 and LANES % (chans // groups) == 0
    if n == SIDES * LAYERS and whole_heads and fits:
        return layered(streams, filters, gain)
    return local(streams, filters, gain)


def solution(mesh):
    placed = (P(None, "ctx", "grp"), P(None, "grp", None), P("grp"))
    return jax.shard_map(
        chosen, mesh=mesh, in_specs=placed, out_specs=P("ctx", "grp"), check_vma=False
    )
```

```python
import functools
import math

import jax
import jax.numpy as jnp
import numpy as np
from jax import lax
from jax.experimental import pallas as pl
from jax.experimental.pallas import tpu as pltpu
from jax.sharding import PartitionSpec as P

HD = 128
LANES = 128
MESH = pl.DeviceIdType.MESH
SIDES = 2
LAYERS = 4
HUB = 1


def layered_kernel(
    n,
    n_grp,
    streams,
    filters,
    gain,
    out,
    buf,
    turned,
    toep,
    feat,
    far_kv,
    far_q,
    part,
    part_stat,
    inbox,
    in_stat,
    own_acc,
    own_top,
    own_total,
    sending,
    att,
    sums,
    local_sem,
    side_send,
    side_recv,
    halo_send,
    halo_recv,
    kv_send,
    kv_recv,
    q_send,
    q_recv,
    part_send,
    part_recv,
    stat_send,
    stat_recv,
    back_send,
    back_recv,
    sum_send,
    sum_recv,
):
    me = lax.axis_index("ctx")
    my_grp = lax.axis_index("grp")
    layer = me // SIDES
    side = lax.rem(me, SIDES)
    other = 1 - side
    rows = streams.shape[1]
    chans = streams.shape[2]
    groups = filters.shape[1]
    flen = filters.shape[2]
    half = chans // SIDES
    heads = half // HD
    span = rows * SIDES
    width = chans // groups
    per_tile = LANES // width
    factor = HD ** (-0.5) * math.log2(math.e)

    def place(z, y):
        return {"ctx": z * SIDES + y}

    def lanes_of(h):
        return pl.ds(pl.multiple_of(h * HD, HD), HD)

    def half_lanes(y, h):
        return pl.ds(pl.multiple_of(y * half + h * HD, HD), HD)

    def remote(src, dst, send, recv, device):
        return pltpu.make_async_remote_copy(
            src_ref=src,
            dst_ref=dst,
            send_sem=send,
            recv_sem=recv,
            device_id=device,
            device_id_type=MESH,
        )

    def own_copy():
        start = pl.multiple_of(flen + side * rows, flen)
        return pltpu.make_async_copy(
            streams.at[:, :, pl.ds(pl.multiple_of(side * half, HD), half)],
            buf.at[:, pl.ds(start, rows), :],
            local_sem.at[0],
        )

    spans = ((rows - flen, flen), (0, rows - flen))

    def side_copy(s, h, p):
        first, size = spans[p]
        start = pl.multiple_of(flen + side * rows + first, flen)
        return remote(
            streams.at[s, pl.ds(first, size), half_lanes(other, h)],
            buf.at[s, pl.ds(start, size), lanes_of(h)],
            side_send.at[s, h, p],
            side_recv.at[s, h, p],
            place(layer, other),
        )

    def halo_copy(s, h):
        return remote(
            buf.at[s, pl.ds(span, flen), lanes_of(h)],
            buf.at[s, pl.ds(0, flen), lanes_of(h)],
            halo_send.at[s, h],
            halo_recv.at[s, h],
            place(lax.rem(layer + 1, LAYERS), side),
        )

    def own_halo_copy(s, h):
        return remote(
            streams.at[s, pl.ds(rows - flen, flen), half_lanes(side, h)],
            buf.at[s, pl.ds(0, flen), lanes_of(h)],
            halo_send.at[s, h],
            halo_recv.at[s, h],
            place(lax.rem(layer + 1, LAYERS), side),
        )

    def rows_of(r):
        return pl.ds(pl.multiple_of(r * rows, flen), rows)

    def kv_copy(j, h, r):
        return remote(
            feat.at[1 + j, rows_of(r), lanes_of(h)],
            far_kv.at[j, rows_of(r), lanes_of(h)],
            kv_send.at[j, h, r],
            kv_recv.at[j, h, r],
            place(HUB, side),
        )

    def q_copy(d, h):
        return remote(
            feat.at[0, :, lanes_of(h)],
            far_q.at[d, :, lanes_of(h)],
            q_send.at[d, h],
            q_recv.at[d, h],
            place(lax.rem(layer + LAYERS - d - 1, LAYERS), side),
        )

    def part_copy(d, h, r):
        return remote(
            part.at[d, rows_of(r), lanes_of(h)],
            inbox.at[d, rows_of(r), lanes_of(h)],
            part_send.at[d, h, r],
            part_recv.at[d, h, r],
            place(lax.rem(layer + d + 1, LAYERS), side),
        )

    def stat_copy(d, h, r):
        return remote(
            part_stat.at[d, h, r, pl.ds(0, 2)],
            in_stat.at[d, h, r, pl.ds(0, 2)],
            stat_send.at[d, h, r],
            stat_recv.at[d, h, r],
            place(lax.rem(layer + d + 1, LAYERS), side),
        )

    def back_copy(h, y):
        return remote(
            sending.at[:, lanes_of(h)],
            att.at[:, half_lanes(y, h)],
            back_send.at[h],
            back_recv.at[h],
            place(layer, other),
        )

    barrier = pltpu.get_barrier_semaphore()

    def greet(device):
        pl.semaphore_signal(barrier, inc=1, device_id=device, device_id_type=MESH)

    greet(place(layer, other))
    for k in range(1, LAYERS):
        partner = lax.rem(layer + k, LAYERS)

        @pl.when((partner == HUB) | (layer == HUB) | ((partner > 0) & (layer > 0)))
        def _():
            greet(place(partner, side))

    for k in range(1, n_grp):
        greet({"grp": lax.rem(my_grp + k, n_grp)})
    partners = jnp.where(layer == 0, 1, jnp.where(layer == HUB, LAYERS - 1, LAYERS - 2))
    own_copy().start()
    pl.semaphore_wait(barrier, partners + n_grp)

    last = layer == LAYERS - 1
    sends_own_halo = (side == SIDES - 1) & jnp.logical_not(last)
    passes_halo = (side < SIDES - 1) & jnp.logical_not(last)

    def send_side(s, h):
        for p in range(2):
            side_copy(s, h, p).start()

    @pl.when(layer == 0)
    def _():
        @pl.loop(0, heads)
        def _(h):
            send_side(1, h)
            send_side(2, h)
            side_copy(0, h, 0).start()

        @pl.loop(0, heads)
        def _(h):
            side_copy(0, h, 1).start()

    @pl.when(layer == HUB)
    def _():
        @pl.loop(0, heads)
        def _(h):
            side_copy(0, h, 0).start()

        @pl.loop(0, heads)
        def _(h):
            for s in (1, 2):
                side_copy(s, h, 0).start()

        @pl.loop(0, heads)
        def _(h):
            for s in (1, 2, 0):
                side_copy(s, h, 1).start()

    @pl.when(layer > HUB)
    def _():
        @pl.loop(0, heads)
        def _(h):
            send_side(0, h)

        @pl.loop(0, heads)
        def _(h):
            for s in (1, 2):
                side_copy(s, h, 0).start()

        @pl.loop(0, heads)
        def _(h):
            for s in (1, 2):
                side_copy(s, h, 1).start()

    @pl.when(sends_own_halo & (layer == 0))
    def _():
        for s in range(3):
            own_halo_copy(s, 0).start()

    @pl.when(sends_own_halo & (layer > 0))
    def _():
        @pl.loop(0, heads)
        def _(h):
            own_halo_copy(0, h).start()

        @pl.loop(0, heads)
        def _(h):
            own_halo_copy(1, h).start()
            own_halo_copy(2, h).start()

    @pl.when(layer == 0)
    def _():
        for s in range(3):
            buf[s, pl.ds(0, flen), :] = jnp.zeros((flen, half), buf.dtype)

    own_groups = half // width
    row_id = lax.broadcasted_iota(jnp.int32, (flen, flen), 0)
    col_id = lax.broadcasted_iota(jnp.int32, (flen, flen), 1)
    flip = jnp.where(
        (row_id + col_id == flen) | ((row_id == 0) & (col_id == 0)), 1.0, 0.0
    ).astype(jnp.bfloat16)
    for s in range(3):
        turned[s] = jnp.dot(
            filters[s, pl.ds(pl.multiple_of(side * own_groups, own_groups), own_groups), :],
            flip,
            preferred_element_type=jnp.float32,
        )

    def build(s, h):
        lines = turned[s, pl.ds(pl.multiple_of(h * per_tile, per_tile), per_tile), :]
        for g in range(per_tile):
            table = pltpu.roll(
                jnp.broadcast_to(lines[g : g + 1], (flen, flen)), 0, 1, stride=1, stride_axis=0
            )
            lower = jnp.where(col_id <= row_id, table, 0.0)
            upper = jnp.where(col_id > row_id, table, 0.0)
            where = pl.ds(g * flen, flen)
            toep[where, pl.ds(0, flen)] = upper.astype(toep.dtype)
            toep[where, pl.ds(flen, flen)] = lower.astype(toep.dtype)

    blocks = span // flen
    lane_group = lax.broadcasted_iota(jnp.int32, (flen, blocks * LANES), 1)
    lane_group = lax.rem(lane_group, LANES) // width

    def fold(values, op):
        result = values[:, :LANES]
        for c in range(1, values.shape[1] // LANES):
            result = op(result, values[:, c * LANES : (c + 1) * LANES])
        return result

    def filter_rows(s, h, first, count):
        lanes = lanes_of(h)
        starts = [pl.multiple_of(first + b * flen, flen) for b in range(count)]
        window = [buf[s, pl.ds(start, 2 * flen), lanes] for start in starts]
        product = jnp.dot(
            toep[...], jnp.concatenate(window, axis=1), preferred_element_type=jnp.float32
        )
        result = product[:flen]
        group = lane_group[:, : count * LANES]
        for g in range(1, per_tile):
            result = jnp.where(group == g, product[g * flen : (g + 1) * flen], result)
        result = result.astype(feat.dtype)
        for b, start in enumerate(starts):
            feat[s, pl.ds(start, flen), lanes] = result[:, b * LANES : (b + 1) * LANES]

    def take_tail(s, h):
        side_copy(s, h, 0).wait_recv()

        @pl.when(passes_halo)
        def _():
            halo_copy(s, h).start()

    def step(s, h, tail=True):
        build(s, h)
        if tail:
            take_tail(s, h)
        side_copy(s, h, 1).wait_recv()

        @pl.when(layer > 0)
        def _():
            halo_copy(s, h).wait_recv()

        filter_rows(s, h, 0, blocks)

    def attend(query, pieces):
        parts = []
        for key, _, last in pieces:
            block = lax.dot_general(
                query, key, (((1,), (1,)), ((), ())), preferred_element_type=jnp.float32
            )
            if last:
                line = lax.broadcasted_iota(jnp.int32, block.shape, 0)
                spot = lax.broadcasted_iota(jnp.int32, block.shape, 1)
                block = jnp.where(spot <= line, block, -1e30)
            parts.append(block)
        top = functools.reduce(jnp.maximum, [fold(p, jnp.maximum) for p in parts])
        top = jnp.max(top, axis=1, keepdims=True)
        weights = [jnp.exp2((p - top) * factor) for p in parts]
        total = functools.reduce(jnp.add, [fold(w, jnp.add) for w in weights])
        total = jnp.sum(total, axis=1, keepdims=True)
        mixed = [
            jnp.dot(w.astype(jnp.bfloat16), p[1], preferred_element_type=jnp.float32)
            for w, p in zip(weights, pieces)
        ]
        return functools.reduce(jnp.add, mixed), top, total

    def piece(ref, base, h, first, size, last=False):
        where = pl.ds(first, size)
        return (ref[base, where, lanes_of(h)], ref[base + 1, where, lanes_of(h)], last)

    def own_pieces(h, r):
        before = [piece(feat, 1, h, 0, r * rows)] if r else []
        return before + [piece(feat, 1, h, r * rows, rows, True)]

    def query_of(h, r):
        return feat[0, pl.ds(r * rows, rows), lanes_of(h)]

    def finish(h, values):
        for r in range(SIDES):
            @pl.when(side == r)
            def _():
                att[:, half_lanes(side, h)] = values[r]
                sending[:, lanes_of(h)] = values[1 - r]

    lane_id = lax.broadcasted_iota(jnp.int32, (rows, LANES), 1)

    def serve(count, h, pieces):
        for d in range(count):
            q_copy(d, h).wait_recv()

        @pl.loop(0, SIDES)
        def _(i):
            r = lax.rem(other + i, SIDES)
            results = [
                attend(far_q[d, rows_of(r), lanes_of(h)], pieces) for d in range(count)
            ]
            for d, (mixed, top, total) in reversed(list(enumerate(results))):
                part[d, rows_of(r), lanes_of(h)] = (mixed / total).astype(part.dtype)
                part_stat[d, h, r] = jnp.where(lane_id == 0, top, total).T[:8]
                part_copy(d, h, r).start()
                stat_copy(d, h, r).start()

    def keep(h):
        for r in range(SIDES):
            mixed, top, total = attend(query_of(h, r), own_pieces(h, r))
            own_acc[h, r] = mixed
            own_top[h, r] = jnp.broadcast_to(top, (rows, LANES))
            own_total[h, r] = jnp.broadcast_to(total, (rows, LANES))

    def spread(line):
        return jnp.broadcast_to(line, (LANES, rows)).T

    def merge(h, count):
        @pl.loop(0, SIDES)
        def _(i):
            r = lax.rem(other + i, SIDES)
            for d in range(count):
                part_copy(d, h, r).wait_recv()
                stat_copy(d, h, r).wait_recv()
            tops = [own_top[h, r]] + [spread(in_stat[d, h, r, 0:1, :]) for d in range(count)]
            totals = [own_total[h, r]] + [spread(in_stat[d, h, r, 1:2, :]) for d in range(count)]
            top = functools.reduce(jnp.maximum, tops)
            scales = [jnp.exp2((t - top) * factor) for t in tops]
            total = functools.reduce(jnp.add, [a * b for a, b in zip(scales, totals)])
            mixed = own_acc[h, r] * scales[0]
            for d in range(count):
                values = inbox[d, rows_of(r), lanes_of(h)].astype(jnp.float32)
                mixed = mixed + values * (scales[d + 1] * totals[d + 1])
            values = (mixed / total).astype(jnp.bfloat16)

            @pl.when(i == 0)
            def _():
                sending[:, lanes_of(h)] = values
                back_copy(h, side).start()

            @pl.when(i > 0)
            def _():
                att[:, half_lanes(side, h)] = values

    own_copy().wait()

    @pl.when(layer == 0)
    def _():
        @pl.loop(0, heads)
        def _(h):
            @pl.loop(0, 2)
            def _(j):
                build(1 + j, h)

                @pl.loop(0, SIDES)
                def _(i):
                    r = lax.rem(side + i, SIDES)

                    @pl.when(i != side)
                    def _():
                        take_tail(1 + j, h)

                    @pl.when(i > 0)
                    def _():
                        side_copy(1 + j, h, 1).wait_recv()

                    filter_rows(1 + j, h, r * rows, rows // flen)
                    kv_copy(j, h, r).start()

            take_tail(0, h)

            @pl.when((side == SIDES - 1) & (h + 1 < heads))
            def _():
                for s in range(3):
                    own_halo_copy(s, h + 1).start()

        @pl.loop(0, heads)
        def _(h):
            step(0, h, False)
            results = [attend(query_of(h, r), own_pieces(h, r)) for r in range(SIDES)]
            finish(h, [(mixed / total).astype(jnp.bfloat16) for mixed, _, total in results])
            back_copy(h, side).start()

    @pl.when(layer == HUB)
    def _():
        @pl.loop(0, heads)
        def _(h):
            take_tail(0, h)

        @pl.loop(0, heads)
        def _(h):
            for j in range(2):
                take_tail(1 + j, h)

        @pl.loop(0, heads)
        def _(h):
            @pl.loop(0, 2)
            def _(j):
                step(1 + j, h, False)

            for j in range(2):
                for r in range(SIDES):
                    kv_copy(j, h, r).wait_recv()

            serve(
                LAYERS - 1 - HUB, h, [piece(far_kv, 0, h, 0, span), piece(feat, 1, h, 0, span)]
            )

            step(0, h, False)
            far = piece(far_kv, 0, h, 0, span)
            results = [attend(query_of(h, r), [far] + own_pieces(h, r)) for r in range(SIDES)]
            finish(h, [(mixed / total).astype(jnp.bfloat16) for mixed, _, total in results])
            back_copy(h, side).start()

    @pl.when(layer > HUB)
    def _():
        @pl.loop(0, heads)
        def _(h):
            step(0, h)

            @pl.when(last)
            def _():
                q_copy(1, h).start()

            q_copy(0, h).start()

        @pl.loop(0, heads)
        def _(h):
            for j in range(2):
                take_tail(1 + j, h)

        @pl.loop(0, heads)
        def _(h):
            @pl.loop(0, 2)
            def _(j):
                step(1 + j, h, False)

            keep(h)

            @pl.when(jnp.logical_not(last))
            def _():
                serve(1, h, [piece(feat, 1, h, 0, span)])

    @pl.when(layer == LAYERS - 2)
    def _():
        @pl.loop(0, heads)
        def _(h):
            merge(h, 1)

    @pl.when(layer == LAYERS - 1)
    def _():
        @pl.loop(0, heads)
        def _(h):
            merge(h, 2)

    @pl.loop(0, heads)
    def _(h):
        back_copy(h, side).wait_recv()

    row_blocks = rows // flen

    @pl.loop(0, row_blocks)
    def _(b):
        where = pl.ds(pl.multiple_of(b * flen, flen), flen)
        wide = att[where, :].astype(jnp.float32)
        squares = fold(wide * wide, jnp.add).T
        squares = squares.reshape(LANES // 8, 8, flen)
        sums[0, :, where] = jnp.sum(squares, axis=0)

    def sum_copy(k):
        return remote(
            sums.at[0],
            sums.at[k],
            sum_send.at[k],
            sum_recv.at[k],
            {"grp": lax.rem(my_grp + k, n_grp)},
        )

    for k in range(1, n_grp):
        sum_copy(k).start()
    for k in range(1, n_grp):
        sum_copy(k).wait()

    @pl.loop(0, row_blocks)
    def _(b):
        where = pl.ds(pl.multiple_of(b * flen, flen), flen)
        power = sums[0, :, where]
        for k in range(1, n_grp):
            power = power + sums[k, :, where]
        power = jnp.sum(power, axis=0, keepdims=True) / (chans * n_grp)
        power = jnp.broadcast_to(lax.rsqrt(power + 1e-06), (LANES, flen)).T
        wide = att[where, :].astype(jnp.float32)
        for c in range(chans // LANES):
            lanes = slice(c * LANES, (c + 1) * LANES)
            out[where, lanes] = (wide[:, lanes] * gain[:, lanes] * power).astype(out.dtype)

    @pl.loop(0, heads)
    def _(h):
        for s in range(3):
            for p in range(2):
                side_copy(s, h, p).wait_send()
        back_copy(h, side).wait_send()

        @pl.when(jnp.logical_not(last))
        def _():
            for s in range(3):
                halo_copy(s, h).wait_send()

        @pl.when(layer == 0)
        def _():
            for j in range(2):
                for r in range(SIDES):
                    kv_copy(j, h, r).wait_send()

        @pl.when(layer > HUB)
        def _():
            q_copy(0, h).wait_send()

        @pl.when(layer == LAYERS - 1)
        def _():
            q_copy(1, h).wait_send()

        @pl.when((layer >= HUB) & (layer < LAYERS - 1))
        def _():
            for r in range(SIDES):
                part_copy(0, h, r).wait_send()
                stat_copy(0, h, r).wait_send()

        @pl.when(layer == HUB)
        def _():
            for r in range(SIDES):
                part_copy(1, h, r).wait_send()
                stat_copy(1, h, r).wait_send()


def layered(streams, filters, gain):
    n, n_grp = lax.axis_size("ctx"), lax.axis_size("grp")
    _, rows, chans = streams.shape
    _, groups, flen = filters.shape
    half = chans // SIDES
    heads = half // HD
    span = rows * SIDES
    per_tile = LANES * groups // chans
    vmem = pl.BlockSpec(memory_space=pltpu.VMEM)
    dma = pltpu.SemaphoreType.DMA
    low = jnp.bfloat16
    far = LAYERS - 1 - HUB
    return pl.pallas_call(
        functools.partial(layered_kernel, n, n_grp),
        out_shape=jax.ShapeDtypeStruct((rows, chans), low),
        in_specs=[pl.BlockSpec(memory_space=pl.ANY), vmem, vmem],
        out_specs=vmem,
        scratch_shapes=[
            pltpu.VMEM((3, flen + span, half), low),
            pltpu.VMEM((3, groups // SIDES, flen), jnp.float32),
            pltpu.VMEM((per_tile * flen, 2 * flen), low),
            pltpu.VMEM((3, span, half), low),
            pltpu.VMEM((2, span, half), low),
            pltpu.VMEM((far, span, half), low),
            pltpu.VMEM((far, span, half), low),
            pltpu.VMEM((far, heads, SIDES, 8, rows), jnp.float32),
            pltpu.VMEM((far, span, half), low),
            pltpu.VMEM((far, heads, SIDES, 8, rows), jnp.float32),
            pltpu.VMEM((heads, SIDES, rows, HD), jnp.float32),
            pltpu.VMEM((heads, SIDES, rows, LANES), jnp.float32),
            pltpu.VMEM((heads, SIDES, rows, LANES), jnp.float32),
            pltpu.VMEM((rows, half), low),
            pltpu.VMEM((rows, chans), low),
            pltpu.VMEM((n_grp, 8, rows), jnp.float32),
            dma((1,)),
            dma((3, heads, 2)),
            dma((3, heads, 2)),
            dma((3, heads)),
            dma((3, heads)),
            dma((2, heads, SIDES)),
            dma((2, heads, SIDES)),
            dma((far, heads)),
            dma((far, heads)),
            dma((far, heads, SIDES)),
            dma((far, heads, SIDES)),
            dma((far, heads, SIDES)),
            dma((far, heads, SIDES)),
            dma((heads,)),
            dma((heads,)),
            dma((n_grp,)),
            dma((n_grp,)),
        ],
        compiler_params=pltpu.CompilerParams(
            collective_id=0, has_side_effects=True, vmem_limit_bytes=56 * 2**20
        ),
        name="layered",
    )(streams, filters, gain.reshape(1, chans))


def passed_along(block, axis, distance):
    devices = range(lax.axis_size(axis))
    route = [(i - distance, i) for i in devices if i - distance in devices]
    return lax.ppermute(block, axis, route)


def filter_all(streams, filters):
    tok_rows = streams.shape[1]
    chan_count = streams.shape[2]
    filt_len = filters.shape[2]
    group_count = filters.shape[1]
    group_width = chan_count // group_count
    tail = streams[:, tok_rows - filt_len :, :]
    before = passed_along(tail, "ctx", 1)
    padded = jnp.concatenate([before, streams], axis=1)
    block_count = tok_rows // filt_len
    blocks = padded.reshape(3, block_count + 1, filt_len, group_count, group_width)
    zeros = jnp.zeros_like(filters)
    line = jnp.concatenate([zeros[..., :1], filters[..., ::-1], zeros], axis=2)
    table = jnp.broadcast_to(line[:, :, None, :], line.shape[:2] + (filt_len, line.shape[2]))
    table = table.reshape(3, group_count, -1)[..., : 2 * filt_len * filt_len]
    table = table.reshape(3, group_count, filt_len, 2 * filt_len)
    upper, lower = table[..., :filt_len], table[..., filt_len:]
    result = jnp.einsum(
        "agts,absgc->abtgc", lower, blocks[:, 1:], preferred_element_type=jnp.float32
    )
    result = result + jnp.einsum(
        "agts,absgc->abtgc", upper, blocks[:, :-1], preferred_element_type=jnp.float32
    )
    return result.reshape(3, tok_rows, chan_count).astype(jnp.bfloat16)


def attend(queries, positions, keyed, valued):
    tok_rows, chan_count = queries.shape
    head_count = chan_count // HD
    scale = HD ** (-0.5)
    query_heads = queries.reshape(tok_rows, head_count, HD)
    query_last = jnp.max(positions)
    start_state = (
        jnp.full((head_count, tok_rows), -1e30, jnp.float32),
        jnp.zeros((head_count, tok_rows), jnp.float32),
        jnp.zeros((tok_rows, head_count, HD), jnp.float32),
    )
    key_piece = lax.all_gather(keyed, "ctx", axis=0, tiled=True)
    value_piece = lax.all_gather(valued, "ctx", axis=0, tiled=True)
    piece_len = key_piece.shape[0]
    block_len = math.gcd(piece_len, 512)

    def step_block(step_idx, state):
        offset = step_idx * block_len
        key_block = lax.dynamic_slice_in_dim(key_piece, offset, block_len, 0).reshape(
            block_len, head_count, HD
        )
        value_block = lax.dynamic_slice_in_dim(value_piece, offset, block_len, 0).reshape(
            block_len, head_count, HD
        )
        key_pos = offset + jnp.arange(block_len, dtype=jnp.int32)

        def update_block(inner):
            running, totals, accum = inner
            scores = (
                jnp.einsum(
                    "shd,khd->hsk", query_heads, key_block, preferred_element_type=jnp.float32
                )
                * scale
            )
            causal = key_pos[None, None, :] <= positions[None, :, None]
            newtop = jnp.maximum(running, jnp.max(jnp.where(causal, scores, -1e30), axis=2))
            weights = jnp.where(causal, jnp.exp(scores - newtop[:, :, None]), 0.0)
            factor = jnp.exp(running - newtop)
            totals = totals * factor + jnp.sum(weights, axis=2)
            accum = accum * factor.T[:, :, None] + jnp.einsum(
                "hsk,khd->shd",
                weights.astype(jnp.bfloat16),
                value_block,
                preferred_element_type=jnp.float32,
            )
            return (newtop, totals, accum)

        return lax.cond(offset > query_last, lambda inner: inner, update_block, state)

    running, totals, accum = lax.fori_loop(0, piece_len // block_len, step_block, start_state)
    return (accum / totals.T[:, :, None]).reshape(tok_rows, chan_count).astype(jnp.bfloat16)


def local(streams, filters, gain):
    features = filter_all(streams, filters)
    tok_rows = streams.shape[1]
    my_index = lax.axis_index("ctx")
    queries = features[0]
    positions = my_index * tok_rows + jnp.arange(tok_rows, dtype=jnp.int32)
    attended = attend(queries, positions, features[1], features[2])
    wide = attended.astype(jnp.float32)
    power = lax.psum(jnp.sum(wide * wide, axis=1), "grp") / (streams.shape[2] * lax.axis_size("grp"))
    return (wide * gain[None, :] * lax.rsqrt(power + 1e-06)[:, None]).astype(jnp.bfloat16)


def chosen(streams, filters, gain):
    n = lax.axis_size("ctx")
    _, rows, chans = streams.shape
    _, groups, flen = filters.shape
    whole_heads = chans % (SIDES * HD) == 0
    fits = flen == LANES and rows % flen == 0 and LANES % (chans // groups) == 0
    if n == SIDES * LAYERS and whole_heads and fits:
        return layered(streams, filters, gain)
    return local(streams, filters, gain)


def solution(mesh):
    placed = (P(None, "ctx", "grp"), P(None, "grp", None), P("grp"))
    return jax.shard_map(
        chosen, mesh=mesh, in_specs=placed, out_specs=P("ctx", "grp"), check_vma=False
    )
```

```python
import functools
import math

import jax
import jax.numpy as jnp
import numpy as np
from jax import lax
from jax.experimental import pallas as pl
from jax.experimental.pallas import tpu as pltpu
from jax.sharding import PartitionSpec as P

HD = 128
LANES = 128
MESH = pl.DeviceIdType.MESH
SIDES = 2
LAYERS = 4
HUB = 1
FAR = LAYERS - 1 - HUB


def layered_kernel(
    n,
    n_grp,
    streams,
    filters,
    gain,
    out,
    buf,
    turned,
    toep,
    feat,
    far_kv,
    far_q,
    part,
    part_stat,
    inbox,
    in_stat,
    own_acc,
    own_top,
    own_total,
    sending,
    att,
    sums,
    local_sem,
    side_send,
    side_recv,
    halo_send,
    halo_recv,
    kv_send,
    kv_recv,
    q_send,
    q_recv,
    part_send,
    part_recv,
    stat_send,
    stat_recv,
    back_send,
    back_recv,
    sum_send,
    sum_recv,
):
    me = lax.axis_index("ctx")
    my_grp = lax.axis_index("grp")
    layer = me // SIDES
    side = lax.rem(me, SIDES)
    other = 1 - side
    rows = streams.shape[1]
    chans = streams.shape[2]
    groups = filters.shape[1]
    flen = filters.shape[2]
    half = chans // SIDES
    heads = half // HD
    span = rows * SIDES
    width = chans // groups
    per_tile = LANES // width
    factor = HD ** (-0.5) * math.log2(math.e)

    def place(z, y):
        return {"ctx": z * SIDES + y}

    def lanes_of(h):
        return pl.ds(pl.multiple_of(h * HD, HD), HD)

    def half_lanes(y, h):
        return pl.ds(pl.multiple_of(y * half + h * HD, HD), HD)

    def remote(src, dst, send, recv, device):
        return pltpu.make_async_remote_copy(
            src_ref=src,
            dst_ref=dst,
            send_sem=send,
            recv_sem=recv,
            device_id=device,
            device_id_type=MESH,
        )

    def own_copy():
        start = pl.multiple_of(flen + side * rows, flen)
        return pltpu.make_async_copy(
            streams.at[:, :, pl.ds(pl.multiple_of(side * half, HD), half)],
            buf.at[:, pl.ds(start, rows), :],
            local_sem.at[0],
        )

    spans = ((rows - flen, flen), (0, rows - flen))

    def side_copy(s, h, p):
        first, size = spans[p]
        start = pl.multiple_of(flen + side * rows + first, flen)
        return remote(
            streams.at[s, pl.ds(first, size), half_lanes(other, h)],
            buf.at[s, pl.ds(start, size), lanes_of(h)],
            side_send.at[s, h, p],
            side_recv.at[s, h, p],
            place(layer, other),
        )

    def halo_copy(s, h):
        return remote(
            buf.at[s, pl.ds(span, flen), lanes_of(h)],
            buf.at[s, pl.ds(0, flen), lanes_of(h)],
            halo_send.at[s, h],
            halo_recv.at[s, h],
            place(lax.rem(layer + 1, LAYERS), side),
        )

    def own_halo_copy(s, h):
        return remote(
            streams.at[s, pl.ds(rows - flen, flen), half_lanes(side, h)],
            buf.at[s, pl.ds(0, flen), lanes_of(h)],
            halo_send.at[s, h],
            halo_recv.at[s, h],
            place(lax.rem(layer + 1, LAYERS), side),
        )

    def rows_of(r):
        return pl.ds(pl.multiple_of(r * rows, flen), rows)

    def kv_copy(j, h, r):
        return remote(
            feat.at[1 + j, rows_of(r), lanes_of(h)],
            far_kv.at[j, rows_of(r), lanes_of(h)],
            kv_send.at[j, h, r],
            kv_recv.at[j, h, r],
            place(HUB, side),
        )

    def q_copy(d, h):
        return remote(
            feat.at[0, :, lanes_of(h)],
            far_q.at[d, :, lanes_of(h)],
            q_send.at[d, h],
            q_recv.at[d, h],
            place(lax.rem(layer + LAYERS - d - 1, LAYERS), side),
        )

    def part_copy(d, h, r):
        return remote(
            part.at[d, rows_of(r), lanes_of(h)],
            inbox.at[d, rows_of(r), lanes_of(h)],
            part_send.at[d, h, r],
            part_recv.at[d, h, r],
            place(lax.rem(layer + d + 1, LAYERS), side),
        )

    def stat_copy(d, h, r):
        return remote(
            part_stat.at[d, h, r, pl.ds(0, 2)],
            in_stat.at[d, h, r, pl.ds(0, 2)],
            stat_send.at[d, h, r],
            stat_recv.at[d, h, r],
            place(lax.rem(layer + d + 1, LAYERS), side),
        )

    def back_copy(h, y):
        return remote(
            sending.at[:, lanes_of(h)],
            att.at[:, half_lanes(y, h)],
            back_send.at[h],
            back_recv.at[h],
            place(layer, other),
        )

    barrier = pltpu.get_barrier_semaphore()

    def greet(device):
        pl.semaphore_signal(barrier, inc=1, device_id=device, device_id_type=MESH)

    greet(place(layer, other))
    for k in range(1, LAYERS):
        partner = lax.rem(layer + k, LAYERS)

        @pl.when((partner == HUB) | (layer == HUB) | ((partner > 0) & (layer > 0)))
        def _():
            greet(place(partner, side))

    for k in range(1, n_grp):
        greet({"grp": lax.rem(my_grp + k, n_grp)})
    partners = jnp.where(layer == 0, 1, jnp.where(layer == HUB, LAYERS - 1, LAYERS - 2))
    own_copy().start()

    @pl.when(layer == 0)
    def _():
        for s in range(3):
            buf[s, pl.ds(0, flen), :] = jnp.zeros((flen, half), buf.dtype)

    own_groups = half // width
    row_id = lax.broadcasted_iota(jnp.int32, (flen, flen), 0)
    col_id = lax.broadcasted_iota(jnp.int32, (flen, flen), 1)
    flip = jnp.where(
        (row_id + col_id == flen) | ((row_id == 0) & (col_id == 0)), 1.0, 0.0
    ).astype(jnp.bfloat16)
    for s in range(3):
        turned[s] = jnp.dot(
            filters[s, pl.ds(pl.multiple_of(side * own_groups, own_groups), own_groups), :],
            flip,
            preferred_element_type=jnp.float32,
        )

    pl.semaphore_wait(barrier, partners + n_grp)

    last = layer == LAYERS - 1
    sends_own_halo = (side == SIDES - 1) & jnp.logical_not(last)
    passes_halo = (side < SIDES - 1) & jnp.logical_not(last)

    def send_side(s, h):
        for p in range(2):
            side_copy(s, h, p).start()

    @pl.when(layer == 0)
    def _():
        @pl.loop(0, heads)
        def _(h):
            send_side(1, h)
            send_side(2, h)
            side_copy(0, h, 0).start()

        @pl.loop(0, heads)
        def _(h):
            side_copy(0, h, 1).start()

    @pl.when(layer == HUB)
    def _():
        @pl.loop(0, heads)
        def _(h):
            side_copy(0, h, 0).start()

        @pl.loop(0, heads)
        def _(h):
            for s in (1, 2):
                side_copy(s, h, 0).start()

        @pl.loop(0, heads)
        def _(h):
            for s in (1, 2, 0):
                side_copy(s, h, 1).start()

    @pl.when(layer > HUB)
    def _():
        @pl.loop(0, heads)
        def _(h):
            send_side(0, h)

        @pl.loop(0, heads)
        def _(h):
            for s in (1, 2):
                side_copy(s, h, 0).start()

        @pl.loop(0, heads)
        def _(h):
            for s in (1, 2):
                side_copy(s, h, 1).start()

    @pl.when(sends_own_halo & (layer == 0))
    def _():
        for s in (1, 2):
            own_halo_copy(s, 0).start()

    @pl.when(sends_own_halo & (layer > 0))
    def _():
        @pl.loop(0, heads)
        def _(h):
            own_halo_copy(0, h).start()

        @pl.loop(0, heads)
        def _(h):
            own_halo_copy(1, h).start()
            own_halo_copy(2, h).start()

    def build(s, h):
        lines = turned[s, pl.ds(pl.multiple_of(h * per_tile, per_tile), per_tile), :]
        for g in range(per_tile):
            table = pltpu.roll(
                jnp.broadcast_to(lines[g : g + 1], (flen, flen)), 0, 1, stride=1, stride_axis=0
            )
            lower = jnp.where(col_id <= row_id, table, 0.0)
            upper = jnp.where(col_id > row_id, table, 0.0)
            where = pl.ds(g * flen, flen)
            toep[where, pl.ds(0, flen)] = upper.astype(toep.dtype)
            toep[where, pl.ds(flen, flen)] = lower.astype(toep.dtype)

    blocks = span // flen
    lane_group = lax.broadcasted_iota(jnp.int32, (flen, blocks * LANES), 1)
    lane_group = lax.rem(lane_group, LANES) // width

    def fold(values, op):
        result = values[:, :LANES]
        for c in range(1, values.shape[1] // LANES):
            result = op(result, values[:, c * LANES : (c + 1) * LANES])
        return result

    def filter_rows(s, h, first, count):
        lanes = lanes_of(h)
        starts = [pl.multiple_of(first + b * flen, flen) for b in range(count)]
        window = [buf[s, pl.ds(start, 2 * flen), lanes] for start in starts]
        product = jnp.dot(
            toep[...], jnp.concatenate(window, axis=1), preferred_element_type=jnp.float32
        )
        result = product[:flen]
        group = lane_group[:, : count * LANES]
        for g in range(1, per_tile):
            result = jnp.where(group == g, product[g * flen : (g + 1) * flen], result)
        result = result.astype(feat.dtype)
        for b, start in enumerate(starts):
            feat[s, pl.ds(start, flen), lanes] = result[:, b * LANES : (b + 1) * LANES]

    def take_tail(s, h):
        side_copy(s, h, 0).wait_recv()

        @pl.when(passes_halo)
        def _():
            halo_copy(s, h).start()

    def pass_query_halo(h):
        take_tail(0, h)

        @pl.when(sends_own_halo)
        def _():
            own_halo_copy(0, h).start()

    def step(s, h, tail=True):
        build(s, h)
        if tail:
            take_tail(s, h)
        side_copy(s, h, 1).wait_recv()

        @pl.when(layer > 0)
        def _():
            halo_copy(s, h).wait_recv()

        filter_rows(s, h, 0, blocks)

    def attend(query, pieces):
        parts = []
        for key, _, last in pieces:
            block = lax.dot_general(
                query, key, (((1,), (1,)), ((), ())), preferred_element_type=jnp.float32
            )
            if last:
                line = lax.broadcasted_iota(jnp.int32, block.shape, 0)
                spot = lax.broadcasted_iota(jnp.int32, block.shape, 1)
                block = jnp.where(spot <= line, block, -1e30)
            parts.append(block)
        top = functools.reduce(jnp.maximum, [fold(p, jnp.maximum) for p in parts])
        top = jnp.max(top, axis=1, keepdims=True)
        weights = [jnp.exp2((p - top) * factor) for p in parts]
        total = functools.reduce(jnp.add, [fold(w, jnp.add) for w in weights])
        total = jnp.sum(total, axis=1, keepdims=True)
        mixed = [
            jnp.dot(w.astype(jnp.bfloat16), p[1], preferred_element_type=jnp.float32)
            for w, p in zip(weights, pieces)
        ]
        return functools.reduce(jnp.add, mixed), top, total

    def piece(ref, base, h, first, size, last=False):
        where = pl.ds(first, size)
        return (ref[base, where, lanes_of(h)], ref[base + 1, where, lanes_of(h)], last)

    def own_pieces(h, r):
        before = [piece(feat, 1, h, 0, r * rows)] if r else []
        return before + [piece(feat, 1, h, r * rows, rows, True)]

    def query_of(h, r):
        return feat[0, pl.ds(r * rows, rows), lanes_of(h)]

    def finish(h, values):
        for r in range(SIDES):
            @pl.when(side == r)
            def _():
                att[:, half_lanes(side, h)] = values[r]
                sending[:, lanes_of(h)] = values[1 - r]

    lane_id = lax.broadcasted_iota(jnp.int32, (rows, LANES), 1)

    def serve(count, h, pieces):
        for d in range(count):
            q_copy(d, h).wait_recv()

        @pl.loop(0, SIDES)
        def _(i):
            r = lax.rem(other + i, SIDES)
            results = [
                attend(far_q[d, rows_of(r), lanes_of(h)], pieces) for d in range(count)
            ]
            for d, (mixed, top, total) in reversed(list(enumerate(results))):
                part[d, rows_of(r), lanes_of(h)] = (mixed / total).astype(part.dtype)
                part_stat[d, h, r] = jnp.where(lane_id == 0, top, total).T[:8]
                part_copy(d, h, r).start()
                stat_copy(d, h, r).start()

    def hub_serve(h):
        for j in range(2):
            for r in range(SIDES):
                kv_copy(j, h, r).wait_recv()
        for d in range(FAR):
            q_copy(d, h).wait_recv()
        pieces = [piece(far_kv, 0, h, 0, span), piece(feat, 1, h, 0, span)]

        def answer(turns):
            results = [
                attend(far_q[d, rows_of(r), lanes_of(h)], pieces) for r, d in turns
            ]
            for (r, d), (mixed, top, total) in zip(turns, results):
                part[d, rows_of(r), lanes_of(h)] = (mixed / total).astype(part.dtype)
                part_stat[d, h, r] = jnp.where(lane_id == 0, top, total).T[:8]
                part_copy(d, h, r).start()
                stat_copy(d, h, r).start()

        answer([(lax.rem(other + i, SIDES), FAR - 1 - d) for i in range(SIDES) for d in range(FAR)])

    def hub_own(h):
        step(0, h, False)
        far = piece(far_kv, 0, h, 0, span)
        results = [attend(query_of(h, r), [far] + own_pieces(h, r)) for r in range(SIDES)]
        finish(h, [(mixed / total).astype(jnp.bfloat16) for mixed, _, total in results])
        back_copy(h, side).start()

    def keep(h):
        for r in range(SIDES):
            mixed, top, total = attend(query_of(h, r), own_pieces(h, r))
            own_acc[h, r] = mixed
            own_top[h, r] = jnp.broadcast_to(top, (rows, LANES))
            own_total[h, r] = jnp.broadcast_to(total, (rows, LANES))

    def spread(line):
        return jnp.broadcast_to(line, (LANES, rows)).T

    def merge(h, count):
        @pl.loop(0, SIDES)
        def _(i):
            r = lax.rem(other + i, SIDES)
            for d in range(count):
                part_copy(d, h, r).wait_recv()
                stat_copy(d, h, r).wait_recv()
            tops = [own_top[h, r]] + [spread(in_stat[d, h, r, 0:1, :]) for d in range(count)]
            totals = [own_total[h, r]] + [spread(in_stat[d, h, r, 1:2, :]) for d in range(count)]
            top = functools.reduce(jnp.maximum, tops)
            scales = [jnp.exp2((t - top) * factor) for t in tops]
            total = functools.reduce(jnp.add, [a * b for a, b in zip(scales, totals)])
            mixed = own_acc[h, r] * scales[0]
            for d in range(count):
                values = inbox[d, rows_of(r), lanes_of(h)].astype(jnp.float32)
                mixed = mixed + values * (scales[d + 1] * totals[d + 1])
            values = (mixed / total).astype(jnp.bfloat16)

            @pl.when(i == 0)
            def _():
                sending[:, lanes_of(h)] = values
                back_copy(h, side).start()

            @pl.when(i > 0)
            def _():
                att[:, half_lanes(side, h)] = values

    own_copy().wait()

    @pl.when(layer == 0)
    def _():
        @pl.loop(0, heads)
        def _(h):
            @pl.loop(0, 2)
            def _(j):
                build(1 + j, h)

                @pl.loop(0, SIDES)
                def _(i):
                    r = lax.rem(side + i, SIDES)

                    @pl.when(i != side)
                    def _():
                        take_tail(1 + j, h)

                    @pl.when(i > 0)
                    def _():
                        side_copy(1 + j, h, 1).wait_recv()

                    filter_rows(1 + j, h, r * rows, rows // flen)
                    kv_copy(j, h, r).start()

            @pl.when(sends_own_halo & (h + 1 < heads))
            def _():
                for s in (1, 2):
                    own_halo_copy(s, h + 1).start()

            @pl.when(h > 0)
            def _():
                pass_query_halo(h - 1)

        pass_query_halo(heads - 1)

        @pl.loop(0, heads)
        def _(h):
            step(0, h, False)
            results = [attend(query_of(h, r), own_pieces(h, r)) for r in range(SIDES)]
            finish(h, [(mixed / total).astype(jnp.bfloat16) for mixed, _, total in results])
            back_copy(h, side).start()

    @pl.when(layer == HUB)
    def _():
        @pl.loop(0, heads)
        def _(h):
            take_tail(0, h)

        @pl.loop(0, heads)
        def _(h):
            for j in range(2):
                take_tail(1 + j, h)

        @pl.loop(0, heads)
        def _(h):
            @pl.loop(0, 2)
            def _(j):
                step(1 + j, h, False)

            hub_serve(h)

            @pl.when(h > 0)
            def _():
                hub_own(h - 1)

        hub_own(heads - 1)

    @pl.when(layer > HUB)
    def _():
        @pl.loop(0, heads)
        def _(h):
            step(0, h)

            q_copy(0, h).start()

            @pl.when(last)
            def _():
                q_copy(1, h).start()

        @pl.loop(0, heads)
        def _(h):
            for j in range(2):
                take_tail(1 + j, h)

        @pl.loop(0, heads)
        def _(h):
            @pl.loop(0, 2)
            def _(j):
                step(1 + j, h, False)

            @pl.when(jnp.logical_not(last))
            def _():
                serve(1, h, [piece(feat, 1, h, 0, span)])

            keep(h)

    @pl.when(layer == LAYERS - 2)
    def _():
        @pl.loop(0, heads)
        def _(h):
            merge(h, 1)

    @pl.when(layer == LAYERS - 1)
    def _():
        @pl.loop(0, heads)
        def _(h):
            merge(h, 2)

    @pl.loop(0, heads)
    def _(h):
        back_copy(h, side).wait_recv()

    row_blocks = rows // flen

    @pl.loop(0, row_blocks)
    def _(b):
        where = pl.ds(pl.multiple_of(b * flen, flen), flen)
        wide = att[where, :].astype(jnp.float32)
        squares = fold(wide * wide, jnp.add).T
        squares = squares.reshape(LANES // 8, 8, flen)
        sums[0, :, where] = jnp.sum(squares, axis=0)

    def sum_copy(k):
        return remote(
            sums.at[0],
            sums.at[k],
            sum_send.at[k],
            sum_recv.at[k],
            {"grp": lax.rem(my_grp + k, n_grp)},
        )

    for k in range(1, n_grp):
        sum_copy(k).start()
    for k in range(1, n_grp):
        sum_copy(k).wait()

    @pl.loop(0, row_blocks)
    def _(b):
        where = pl.ds(pl.multiple_of(b * flen, flen), flen)
        power = sums[0, :, where]
        for k in range(1, n_grp):
            power = power + sums[k, :, where]
        power = jnp.sum(power, axis=0, keepdims=True) / (chans * n_grp)
        power = jnp.broadcast_to(lax.rsqrt(power + 1e-06), (LANES, flen)).T
        wide = att[where, :].astype(jnp.float32)
        for c in range(chans // LANES):
            lanes = slice(c * LANES, (c + 1) * LANES)
            out[where, lanes] = (wide[:, lanes] * gain[:, lanes] * power).astype(out.dtype)

    @pl.loop(0, heads)
    def _(h):
        for s in range(3):
            for p in range(2):
                side_copy(s, h, p).wait_send()
        back_copy(h, side).wait_send()

        @pl.when(jnp.logical_not(last))
        def _():
            for s in range(3):
                halo_copy(s, h).wait_send()

        @pl.when(layer == 0)
        def _():
            for j in range(2):
                for r in range(SIDES):
                    kv_copy(j, h, r).wait_send()

        @pl.when(layer > HUB)
        def _():
            q_copy(0, h).wait_send()

        @pl.when(layer == LAYERS - 1)
        def _():
            q_copy(1, h).wait_send()

        @pl.when((layer >= HUB) & (layer < LAYERS - 1))
        def _():
            for r in range(SIDES):
                part_copy(0, h, r).wait_send()
                stat_copy(0, h, r).wait_send()

        @pl.when(layer == HUB)
        def _():
            for r in range(SIDES):
                part_copy(1, h, r).wait_send()
                stat_copy(1, h, r).wait_send()


def layered(streams, filters, gain):
    n, n_grp = lax.axis_size("ctx"), lax.axis_size("grp")
    _, rows, chans = streams.shape
    _, groups, flen = filters.shape
    half = chans // SIDES
    heads = half // HD
    span = rows * SIDES
    per_tile = LANES * groups // chans
    vmem = pl.BlockSpec(memory_space=pltpu.VMEM)
    dma = pltpu.SemaphoreType.DMA
    low = jnp.bfloat16
    far = FAR
    return pl.pallas_call(
        functools.partial(layered_kernel, n, n_grp),
        out_shape=jax.ShapeDtypeStruct((rows, chans), low),
        in_specs=[pl.BlockSpec(memory_space=pl.ANY), vmem, vmem],
        out_specs=vmem,
        scratch_shapes=[
            pltpu.VMEM((3, flen + span, half), low),
            pltpu.VMEM((3, groups // SIDES, flen), jnp.float32),
            pltpu.VMEM((per_tile * flen, 2 * flen), low),
            pltpu.VMEM((3, span, half), low),
            pltpu.VMEM((2, span, half), low),
            pltpu.VMEM((far, span, half), low),
            pltpu.VMEM((far, span, half), low),
            pltpu.VMEM((far, heads, SIDES, 8, rows), jnp.float32),
            pltpu.VMEM((far, span, half), low),
            pltpu.VMEM((far, heads, SIDES, 8, rows), jnp.float32),
            pltpu.VMEM((heads, SIDES, rows, HD), jnp.float32),
            pltpu.VMEM((heads, SIDES, rows, LANES), jnp.float32),
            pltpu.VMEM((heads, SIDES, rows, LANES), jnp.float32),
            pltpu.VMEM((rows, half), low),
            pltpu.VMEM((rows, chans), low),
            pltpu.VMEM((n_grp, 8, rows), jnp.float32),
            dma((1,)),
            dma((3, heads, 2)),
            dma((3, heads, 2)),
            dma((3, heads)),
            dma((3, heads)),
            dma((2, heads, SIDES)),
            dma((2, heads, SIDES)),
            dma((far, heads)),
            dma((far, heads)),
            dma((far, heads, SIDES)),
            dma((far, heads, SIDES)),
            dma((far, heads, SIDES)),
            dma((far, heads, SIDES)),
            dma((heads,)),
            dma((heads,)),
            dma((n_grp,)),
            dma((n_grp,)),
        ],
        compiler_params=pltpu.CompilerParams(
            collective_id=0, has_side_effects=True, vmem_limit_bytes=56 * 2**20
        ),
        name="layered",
    )(streams, filters, gain.reshape(1, chans))


def passed_along(block, axis, distance):
    devices = range(lax.axis_size(axis))
    route = [(i - distance, i) for i in devices if i - distance in devices]
    return lax.ppermute(block, axis, route)


def filter_all(streams, filters):
    tok_rows = streams.shape[1]
    chan_count = streams.shape[2]
    filt_len = filters.shape[2]
    group_count = filters.shape[1]
    group_width = chan_count // group_count
    tail = streams[:, tok_rows - filt_len :, :]
    before = passed_along(tail, "ctx", 1)
    padded = jnp.concatenate([before, streams], axis=1)
    block_count = tok_rows // filt_len
    blocks = padded.reshape(3, block_count + 1, filt_len, group_count, group_width)
    zeros = jnp.zeros_like(filters)
    line = jnp.concatenate([zeros[..., :1], filters[..., ::-1], zeros], axis=2)
    table = jnp.broadcast_to(line[:, :, None, :], line.shape[:2] + (filt_len, line.shape[2]))
    table = table.reshape(3, group_count, -1)[..., : 2 * filt_len * filt_len]
    table = table.reshape(3, group_count, filt_len, 2 * filt_len)
    upper, lower = table[..., :filt_len], table[..., filt_len:]
    result = jnp.einsum(
        "agts,absgc->abtgc", lower, blocks[:, 1:], preferred_element_type=jnp.float32
    )
    result = result + jnp.einsum(
        "agts,absgc->abtgc", upper, blocks[:, :-1], preferred_element_type=jnp.float32
    )
    return result.reshape(3, tok_rows, chan_count).astype(jnp.bfloat16)


def attend(queries, positions, keyed, valued):
    tok_rows, chan_count = queries.shape
    head_count = chan_count // HD
    scale = HD ** (-0.5)
    query_heads = queries.reshape(tok_rows, head_count, HD)
    query_last = jnp.max(positions)
    start_state = (
        jnp.full((head_count, tok_rows), -1e30, jnp.float32),
        jnp.zeros((head_count, tok_rows), jnp.float32),
        jnp.zeros((tok_rows, head_count, HD), jnp.float32),
    )
    key_piece = lax.all_gather(keyed, "ctx", axis=0, tiled=True)
    value_piece = lax.all_gather(valued, "ctx", axis=0, tiled=True)
    piece_len = key_piece.shape[0]
    block_len = math.gcd(piece_len, 512)

    def step_block(step_idx, state):
        offset = step_idx * block_len
        key_block = lax.dynamic_slice_in_dim(key_piece, offset, block_len, 0).reshape(
            block_len, head_count, HD
        )
        value_block = lax.dynamic_slice_in_dim(value_piece, offset, block_len, 0).reshape(
            block_len, head_count, HD
        )
        key_pos = offset + jnp.arange(block_len, dtype=jnp.int32)

        def update_block(inner):
            running, totals, accum = inner
            scores = (
                jnp.einsum(
                    "shd,khd->hsk", query_heads, key_block, preferred_element_type=jnp.float32
                )
                * scale
            )
            causal = key_pos[None, None, :] <= positions[None, :, None]
            newtop = jnp.maximum(running, jnp.max(jnp.where(causal, scores, -1e30), axis=2))
            weights = jnp.where(causal, jnp.exp(scores - newtop[:, :, None]), 0.0)
            factor = jnp.exp(running - newtop)
            totals = totals * factor + jnp.sum(weights, axis=2)
            accum = accum * factor.T[:, :, None] + jnp.einsum(
                "hsk,khd->shd",
                weights.astype(jnp.bfloat16),
                value_block,
                preferred_element_type=jnp.float32,
            )
            return (newtop, totals, accum)

        return lax.cond(offset > query_last, lambda inner: inner, update_block, state)

    running, totals, accum = lax.fori_loop(0, piece_len // block_len, step_block, start_state)
    return (accum / totals.T[:, :, None]).reshape(tok_rows, chan_count).astype(jnp.bfloat16)


def local(streams, filters, gain):
    features = filter_all(streams, filters)
    tok_rows = streams.shape[1]
    my_index = lax.axis_index("ctx")
    queries = features[0]
    positions = my_index * tok_rows + jnp.arange(tok_rows, dtype=jnp.int32)
    attended = attend(queries, positions, features[1], features[2])
    wide = attended.astype(jnp.float32)
    power = lax.psum(jnp.sum(wide * wide, axis=1), "grp") / (streams.shape[2] * lax.axis_size("grp"))
    return (wide * gain[None, :] * lax.rsqrt(power + 1e-06)[:, None]).astype(jnp.bfloat16)


def chosen(streams, filters, gain):
    n = lax.axis_size("ctx")
    _, rows, chans = streams.shape
    _, groups, flen = filters.shape
    whole_heads = chans % (SIDES * HD) == 0
    fits = flen == LANES and rows % flen == 0 and LANES % (chans // groups) == 0
    if n == SIDES * LAYERS and whole_heads and fits:
        return layered(streams, filters, gain)
    return local(streams, filters, gain)


def solution(mesh):
    placed = (P(None, "ctx", "grp"), P(None, "grp", None), P("grp"))
    return jax.shard_map(
        chosen, mesh=mesh, in_specs=placed, out_specs=P("ctx", "grp"), check_vma=False
    )
```

```python
import functools
import math

import jax
import jax.numpy as jnp
import numpy as np
from jax import lax
from jax.experimental import pallas as pl
from jax.experimental.pallas import tpu as pltpu
from jax.sharding import PartitionSpec as P

HD = 128
LANES = 128
MESH = pl.DeviceIdType.MESH
SIDES = 2
LAYERS = 4
HUB = 1
FAR = LAYERS - 1 - HUB


def layered_kernel(
    n,
    n_grp,
    streams,
    filters,
    gain,
    out,
    buf,
    turned,
    toep,
    feat,
    far_kv,
    far_q,
    part,
    part_stat,
    inbox,
    in_stat,
    own_acc,
    own_top,
    own_total,
    sending,
    att,
    sums,
    local_sem,
    side_send,
    side_recv,
    halo_send,
    halo_recv,
    kv_send,
    kv_recv,
    q_send,
    q_recv,
    part_send,
    part_recv,
    stat_send,
    stat_recv,
    back_send,
    back_recv,
    sum_send,
    sum_recv,
):
    me = lax.axis_index("ctx")
    my_grp = lax.axis_index("grp")
    layer = me // SIDES
    side = lax.rem(me, SIDES)
    other = 1 - side
    rows = streams.shape[1]
    chans = streams.shape[2]
    groups = filters.shape[1]
    flen = filters.shape[2]
    half = chans // SIDES
    heads = half // HD
    span = rows * SIDES
    width = chans // groups
    per_tile = LANES // width
    factor = HD ** (-0.5) * math.log2(math.e)

    def place(z, y):
        return {"ctx": z * SIDES + y}

    def lanes_of(h):
        return pl.ds(pl.multiple_of(h * HD, HD), HD)

    def half_lanes(y, h):
        return pl.ds(pl.multiple_of(y * half + h * HD, HD), HD)

    def remote(src, dst, send, recv, device):
        return pltpu.make_async_remote_copy(
            src_ref=src,
            dst_ref=dst,
            send_sem=send,
            recv_sem=recv,
            device_id=device,
            device_id_type=MESH,
        )

    def own_copy():
        start = pl.multiple_of(flen + side * rows, flen)
        return pltpu.make_async_copy(
            streams.at[:, :, pl.ds(pl.multiple_of(side * half, HD), half)],
            buf.at[:, pl.ds(start, rows), :],
            local_sem.at[0],
        )

    spans = ((rows - flen, flen), (0, rows - flen))

    def side_copy(s, h, p):
        first, size = spans[p]
        start = pl.multiple_of(flen + side * rows + first, flen)
        return remote(
            streams.at[s, pl.ds(first, size), half_lanes(other, h)],
            buf.at[s, pl.ds(start, size), lanes_of(h)],
            side_send.at[s, h, p],
            side_recv.at[s, h, p],
            place(layer, other),
        )

    def halo_copy(s, h):
        return remote(
            buf.at[s, pl.ds(span, flen), lanes_of(h)],
            buf.at[s, pl.ds(0, flen), lanes_of(h)],
            halo_send.at[s, h],
            halo_recv.at[s, h],
            place(lax.rem(layer + 1, LAYERS), side),
        )

    def own_halo_copy(s, h):
        return remote(
            streams.at[s, pl.ds(rows - flen, flen), half_lanes(side, h)],
            buf.at[s, pl.ds(0, flen), lanes_of(h)],
            halo_send.at[s, h],
            halo_recv.at[s, h],
            place(lax.rem(layer + 1, LAYERS), side),
        )

    def rows_of(r):
        return pl.ds(pl.multiple_of(r * rows, flen), rows)

    def kv_copy(j, h, r):
        return remote(
            feat.at[1 + j, rows_of(r), lanes_of(h)],
            far_kv.at[j, rows_of(r), lanes_of(h)],
            kv_send.at[j, h, r],
            kv_recv.at[j, h, r],
            place(HUB, side),
        )

    def q_copy(d, h):
        return remote(
            feat.at[0, :, lanes_of(h)],
            far_q.at[d, :, lanes_of(h)],
            q_send.at[d, h],
            q_recv.at[d, h],
            place(lax.rem(layer + LAYERS - d - 1, LAYERS), side),
        )

    def part_copy(d, h, r):
        return remote(
            part.at[d, rows_of(r), lanes_of(h)],
            inbox.at[d, rows_of(r), lanes_of(h)],
            part_send.at[d, h, r],
            part_recv.at[d, h, r],
            place(lax.rem(layer + d + 1, LAYERS), side),
        )

    def stat_copy(d, h, r):
        return remote(
            part_stat.at[d, h, r, pl.ds(0, 2)],
            in_stat.at[d, h, r, pl.ds(0, 2)],
            stat_send.at[d, h, r],
            stat_recv.at[d, h, r],
            place(lax.rem(layer + d + 1, LAYERS), side),
        )

    def back_copy(h, y):
        return remote(
            sending.at[:, lanes_of(h)],
            att.at[:, half_lanes(y, h)],
            back_send.at[h],
            back_recv.at[h],
            place(layer, other),
        )

    barrier = pltpu.get_barrier_semaphore()

    def greet(device):
        pl.semaphore_signal(barrier, inc=1, device_id=device, device_id_type=MESH)

    greet(place(layer, other))
    for k in range(1, LAYERS):
        partner = lax.rem(layer + k, LAYERS)

        @pl.when((partner == HUB) | (layer == HUB) | ((partner > 0) & (layer > 0)))
        def _():
            greet(place(partner, side))

    for k in range(1, n_grp):
        greet({"grp": lax.rem(my_grp + k, n_grp)})
    partners = jnp.where(layer == 0, 1, jnp.where(layer == HUB, LAYERS - 1, LAYERS - 2))
    own_copy().start()

    @pl.when(layer == 0)
    def _():
        for s in range(3):
            buf[s, pl.ds(0, flen), :] = jnp.zeros((flen, half), buf.dtype)

    own_groups = half // width
    row_id = lax.broadcasted_iota(jnp.int32, (flen, flen), 0)
    col_id = lax.broadcasted_iota(jnp.int32, (flen, flen), 1)
    flip = jnp.where(
        (row_id + col_id == flen) | ((row_id == 0) & (col_id == 0)), 1.0, 0.0
    ).astype(jnp.bfloat16)
    for s in range(3):
        turned[s] = jnp.dot(
            filters[s, pl.ds(pl.multiple_of(side * own_groups, own_groups), own_groups), :],
            flip,
            preferred_element_type=jnp.float32,
        )

    pl.semaphore_wait(barrier, partners + n_grp)

    last = layer == LAYERS - 1
    sends_own_halo = (side == SIDES - 1) & jnp.logical_not(last)
    passes_halo = (side < SIDES - 1) & jnp.logical_not(last)

    def send_side(s, h):
        for p in range(2):
            side_copy(s, h, p).start()

    @pl.when(layer == 0)
    def _():
        @pl.loop(0, heads)
        def _(h):
            send_side(1, h)
            send_side(2, h)
            side_copy(0, h, 0).start()

        @pl.loop(0, heads)
        def _(h):
            side_copy(0, h, 1).start()

    @pl.when(layer == HUB)
    def _():
        @pl.loop(0, heads)
        def _(h):
            side_copy(0, h, 0).start()

        @pl.loop(0, heads)
        def _(h):
            for s in (1, 2):
                side_copy(s, h, 0).start()

        @pl.loop(0, heads)
        def _(h):
            for s in (1, 2, 0):
                side_copy(s, h, 1).start()

    @pl.when(layer > HUB)
    def _():
        @pl.loop(0, heads)
        def _(h):
            send_side(0, h)

        @pl.loop(0, heads)
        def _(h):
            for s in (1, 2):
                side_copy(s, h, 0).start()

        @pl.loop(0, heads)
        def _(h):
            for s in (1, 2):
                side_copy(s, h, 1).start()

    @pl.when(sends_own_halo & (layer == 0))
    def _():
        for s in (1, 2):
            own_halo_copy(s, 0).start()

    @pl.when(sends_own_halo & (layer > 0))
    def _():
        @pl.loop(0, heads)
        def _(h):
            own_halo_copy(0, h).start()

        @pl.loop(0, heads)
        def _(h):
            own_halo_copy(1, h).start()
            own_halo_copy(2, h).start()

    def build(s, h):
        lines = turned[s, pl.ds(pl.multiple_of(h * per_tile, per_tile), per_tile), :]
        for g in range(per_tile):
            table = pltpu.roll(
                jnp.broadcast_to(lines[g : g + 1], (flen, flen)), 0, 1, stride=1, stride_axis=0
            )
            lower = jnp.where(col_id <= row_id, table, 0.0)
            upper = jnp.where(col_id > row_id, table, 0.0)
            where = pl.ds(g * flen, flen)
            toep[where, pl.ds(0, flen)] = upper.astype(toep.dtype)
            toep[where, pl.ds(flen, flen)] = lower.astype(toep.dtype)

    blocks = span // flen
    lane_group = lax.broadcasted_iota(jnp.int32, (flen, blocks * LANES), 1)
    lane_group = lax.rem(lane_group, LANES) // width

    def fold(values, op):
        result = values[:, :LANES]
        for c in range(1, values.shape[1] // LANES):
            result = op(result, values[:, c * LANES : (c + 1) * LANES])
        return result

    def filter_rows(s, h, first, count):
        lanes = lanes_of(h)
        starts = [pl.multiple_of(first + b * flen, flen) for b in range(count)]
        window = [buf[s, pl.ds(start, 2 * flen), lanes] for start in starts]
        product = jnp.dot(
            toep[...], jnp.concatenate(window, axis=1), preferred_element_type=jnp.float32
        )
        result = product[:flen]
        group = lane_group[:, : count * LANES]
        for g in range(1, per_tile):
            result = jnp.where(group == g, product[g * flen : (g + 1) * flen], result)
        result = result.astype(feat.dtype)
        for b, start in enumerate(starts):
            feat[s, pl.ds(start, flen), lanes] = result[:, b * LANES : (b + 1) * LANES]

    def take_tail(s, h):
        side_copy(s, h, 0).wait_recv()

        @pl.when(passes_halo)
        def _():
            halo_copy(s, h).start()

    def pass_query_halo(h):
        take_tail(0, h)

        @pl.when(sends_own_halo)
        def _():
            own_halo_copy(0, h).start()

    def step(s, h, tail=True):
        build(s, h)
        if tail:
            take_tail(s, h)
        side_copy(s, h, 1).wait_recv()

        @pl.when(layer > 0)
        def _():
            halo_copy(s, h).wait_recv()

        filter_rows(s, h, 0, blocks)

    def attend(query, pieces):
        parts = []
        for key, _, last in pieces:
            block = lax.dot_general(
                query, key, (((1,), (1,)), ((), ())), preferred_element_type=jnp.float32
            )
            if last:
                line = lax.broadcasted_iota(jnp.int32, block.shape, 0)
                spot = lax.broadcasted_iota(jnp.int32, block.shape, 1)
                block = jnp.where(spot <= line, block, -1e30)
            parts.append(block)
        top = functools.reduce(jnp.maximum, [fold(p, jnp.maximum) for p in parts])
        top = jnp.max(top, axis=1, keepdims=True)
        weights = [jnp.exp2((p - top) * factor) for p in parts]
        total = functools.reduce(jnp.add, [fold(w, jnp.add) for w in weights])
        total = jnp.sum(total, axis=1, keepdims=True)
        mixed = [
            jnp.dot(w.astype(jnp.bfloat16), p[1], preferred_element_type=jnp.float32)
            for w, p in zip(weights, pieces)
        ]
        return functools.reduce(jnp.add, mixed), top, total

    def piece(ref, base, h, first, size, last=False):
        where = pl.ds(first, size)
        return (ref[base, where, lanes_of(h)], ref[base + 1, where, lanes_of(h)], last)

    def own_pieces(h, r):
        before = [piece(feat, 1, h, 0, r * rows)] if r else []
        return before + [piece(feat, 1, h, r * rows, rows, True)]

    def query_of(h, r):
        return feat[0, pl.ds(r * rows, rows), lanes_of(h)]

    def finish(h, values):
        for r in range(SIDES):
            @pl.when(side == r)
            def _():
                att[:, half_lanes(side, h)] = values[r]
                sending[:, lanes_of(h)] = values[1 - r]

    lane_id = lax.broadcasted_iota(jnp.int32, (rows, LANES), 1)

    def serve(count, h, pieces):
        for d in range(count):
            q_copy(d, h).wait_recv()

        @pl.loop(0, SIDES)
        def _(i):
            r = lax.rem(other + i, SIDES)
            results = [
                attend(far_q[d, rows_of(r), lanes_of(h)], pieces) for d in range(count)
            ]
            for d, (mixed, top, total) in reversed(list(enumerate(results))):
                part[d, rows_of(r), lanes_of(h)] = (mixed / total).astype(part.dtype)
                part_stat[d, h, r] = jnp.where(lane_id == 0, top, total).T[:8]
                part_copy(d, h, r).start()
                stat_copy(d, h, r).start()

    def hub_serve(h):
        for j in range(2):
            for r in range(SIDES):
                kv_copy(j, h, r).wait_recv()
        for d in range(FAR):
            q_copy(d, h).wait_recv()
        pieces = [piece(far_kv, 0, h, 0, span), piece(feat, 1, h, 0, span)]

        def answer(turns):
            results = [
                attend(far_q[d, rows_of(r), lanes_of(h)], pieces) for r, d in turns
            ]
            for (r, d), (mixed, top, total) in zip(turns, results):
                part[d, rows_of(r), lanes_of(h)] = (mixed / total).astype(part.dtype)
                part_stat[d, h, r] = jnp.where(lane_id == 0, top, total).T[:8]
                part_copy(d, h, r).start()
                stat_copy(d, h, r).start()

        answer([(lax.rem(other + i, SIDES), (d + i) % FAR) for i in range(SIDES) for d in range(FAR)])

    def hub_own(h):
        step(0, h, False)
        far = piece(far_kv, 0, h, 0, span)
        results = [attend(query_of(h, r), [far] + own_pieces(h, r)) for r in range(SIDES)]
        finish(h, [(mixed / total).astype(jnp.bfloat16) for mixed, _, total in results])
        back_copy(h, side).start()

    def keep(h):
        for r in range(SIDES):
            mixed, top, total = attend(query_of(h, r), own_pieces(h, r))
            own_acc[h, r] = mixed
            own_top[h, r] = jnp.broadcast_to(top, (rows, LANES))
            own_total[h, r] = jnp.broadcast_to(total, (rows, LANES))

    def spread(line):
        return jnp.broadcast_to(line, (LANES, rows)).T

    def merge(h, count):
        @pl.loop(0, SIDES)
        def _(i):
            r = lax.rem(other + i, SIDES)
            for d in range(count):
                part_copy(d, h, r).wait_recv()
                stat_copy(d, h, r).wait_recv()
            tops = [own_top[h, r]] + [spread(in_stat[d, h, r, 0:1, :]) for d in range(count)]
            totals = [own_total[h, r]] + [spread(in_stat[d, h, r, 1:2, :]) for d in range(count)]
            top = functools.reduce(jnp.maximum, tops)
            scales = [jnp.exp2((t - top) * factor) for t in tops]
            total = functools.reduce(jnp.add, [a * b for a, b in zip(scales, totals)])
            mixed = own_acc[h, r] * scales[0]
            for d in range(count):
                values = inbox[d, rows_of(r), lanes_of(h)].astype(jnp.float32)
                mixed = mixed + values * (scales[d + 1] * totals[d + 1])
            values = (mixed / total).astype(jnp.bfloat16)

            @pl.when(i == 0)
            def _():
                sending[:, lanes_of(h)] = values
                back_copy(h, side).start()

            @pl.when(i > 0)
            def _():
                att[:, half_lanes(side, h)] = values

    own_copy().wait()

    @pl.when(layer == 0)
    def _():
        @pl.loop(0, heads)
        def _(h):
            @pl.loop(0, 2)
            def _(j):
                build(1 + j, h)

                @pl.loop(0, SIDES)
                def _(i):
                    r = lax.rem(side + i, SIDES)

                    @pl.when(i != side)
                    def _():
                        take_tail(1 + j, h)

                    @pl.when(i > 0)
                    def _():
                        side_copy(1 + j, h, 1).wait_recv()

                    filter_rows(1 + j, h, r * rows, rows // flen)
                    kv_copy(j, h, r).start()

            @pl.when(sends_own_halo & (h + 1 < heads))
            def _():
                for s in (1, 2):
                    own_halo_copy(s, h + 1).start()

            @pl.when(h > 0)
            def _():
                pass_query_halo(h - 1)

        pass_query_halo(heads - 1)

        @pl.loop(0, heads)
        def _(h):
            step(0, h, False)
            results = [attend(query_of(h, r), own_pieces(h, r)) for r in range(SIDES)]
            finish(h, [(mixed / total).astype(jnp.bfloat16) for mixed, _, total in results])
            back_copy(h, side).start()

    @pl.when(layer == HUB)
    def _():
        @pl.loop(0, heads)
        def _(h):
            take_tail(0, h)

        @pl.loop(0, heads)
        def _(h):
            for j in range(2):
                take_tail(1 + j, h)

        @pl.loop(0, heads)
        def _(h):
            @pl.loop(0, 2)
            def _(j):
                step(1 + j, h, False)

            hub_serve(h)

            @pl.when(h > 0)
            def _():
                hub_own(h - 1)

        hub_own(heads - 1)

    @pl.when(layer > HUB)
    def _():
        @pl.loop(0, heads)
        def _(h):
            step(0, h)

            q_copy(0, h).start()

            @pl.when(last)
            def _():
                q_copy(1, h).start()

        @pl.loop(0, heads)
        def _(h):
            for j in range(2):
                take_tail(1 + j, h)

        @pl.loop(0, heads)
        def _(h):
            @pl.loop(0, 2)
            def _(j):
                step(1 + j, h, False)

            @pl.when(jnp.logical_not(last))
            def _():
                serve(1, h, [piece(feat, 1, h, 0, span)])

            keep(h)

    @pl.when(layer == LAYERS - 2)
    def _():
        @pl.loop(0, heads)
        def _(h):
            merge(h, 1)

    @pl.when(layer == LAYERS - 1)
    def _():
        @pl.loop(0, heads)
        def _(h):
            merge(h, 2)

    @pl.loop(0, heads)
    def _(h):
        back_copy(h, side).wait_recv()

    row_blocks = rows // flen

    @pl.loop(0, row_blocks)
    def _(b):
        where = pl.ds(pl.multiple_of(b * flen, flen), flen)
        wide = att[where, :].astype(jnp.float32)
        squares = fold(wide * wide, jnp.add).T
        squares = squares.reshape(LANES // 8, 8, flen)
        sums[0, :, where] = jnp.sum(squares, axis=0)

    def sum_copy(k):
        return remote(
            sums.at[0],
            sums.at[k],
            sum_send.at[k],
            sum_recv.at[k],
            {"grp": lax.rem(my_grp + k, n_grp)},
        )

    for k in range(1, n_grp):
        sum_copy(k).start()
    for k in range(1, n_grp):
        sum_copy(k).wait()

    @pl.loop(0, row_blocks)
    def _(b):
        where = pl.ds(pl.multiple_of(b * flen, flen), flen)
        power = sums[0, :, where]
        for k in range(1, n_grp):
            power = power + sums[k, :, where]
        power = jnp.sum(power, axis=0, keepdims=True) / (chans * n_grp)
        power = jnp.broadcast_to(lax.rsqrt(power + 1e-06), (LANES, flen)).T
        wide = att[where, :].astype(jnp.float32)
        for c in range(chans // LANES):
            lanes = slice(c * LANES, (c + 1) * LANES)
            out[where, lanes] = (wide[:, lanes] * gain[:, lanes] * power).astype(out.dtype)

    @pl.loop(0, heads)
    def _(h):
        for s in range(3):
            for p in range(2):
                side_copy(s, h, p).wait_send()
        back_copy(h, side).wait_send()

        @pl.when(jnp.logical_not(last))
        def _():
            for s in range(3):
                halo_copy(s, h).wait_send()

        @pl.when(layer == 0)
        def _():
            for j in range(2):
                for r in range(SIDES):
                    kv_copy(j, h, r).wait_send()

        @pl.when(layer > HUB)
        def _():
            q_copy(0, h).wait_send()

        @pl.when(layer == LAYERS - 1)
        def _():
            q_copy(1, h).wait_send()

        @pl.when((layer >= HUB) & (layer < LAYERS - 1))
        def _():
            for r in range(SIDES):
                part_copy(0, h, r).wait_send()
                stat_copy(0, h, r).wait_send()

        @pl.when(layer == HUB)
        def _():
            for r in range(SIDES):
                part_copy(1, h, r).wait_send()
                stat_copy(1, h, r).wait_send()


def layered(streams, filters, gain):
    n, n_grp = lax.axis_size("ctx"), lax.axis_size("grp")
    _, rows, chans = streams.shape
    _, groups, flen = filters.shape
    half = chans // SIDES
    heads = half // HD
    span = rows * SIDES
    per_tile = LANES * groups // chans
    vmem = pl.BlockSpec(memory_space=pltpu.VMEM)
    dma = pltpu.SemaphoreType.DMA
    low = jnp.bfloat16
    far = FAR
    return pl.pallas_call(
        functools.partial(layered_kernel, n, n_grp),
        out_shape=jax.ShapeDtypeStruct((rows, chans), low),
        in_specs=[pl.BlockSpec(memory_space=pl.ANY), vmem, vmem],
        out_specs=vmem,
        scratch_shapes=[
            pltpu.VMEM((3, flen + span, half), low),
            pltpu.VMEM((3, groups // SIDES, flen), jnp.float32),
            pltpu.VMEM((per_tile * flen, 2 * flen), low),
            pltpu.VMEM((3, span, half), low),
            pltpu.VMEM((2, span, half), low),
            pltpu.VMEM((far, span, half), low),
            pltpu.VMEM((far, span, half), low),
            pltpu.VMEM((far, heads, SIDES, 8, rows), jnp.float32),
            pltpu.VMEM((far, span, half), low),
            pltpu.VMEM((far, heads, SIDES, 8, rows), jnp.float32),
            pltpu.VMEM((heads, SIDES, rows, HD), jnp.float32),
            pltpu.VMEM((heads, SIDES, rows, LANES), jnp.float32),
            pltpu.VMEM((heads, SIDES, rows, LANES), jnp.float32),
            pltpu.VMEM((rows, half), low),
            pltpu.VMEM((rows, chans), low),
            pltpu.VMEM((n_grp, 8, rows), jnp.float32),
            dma((1,)),
            dma((3, heads, 2)),
            dma((3, heads, 2)),
            dma((3, heads)),
            dma((3, heads)),
            dma((2, heads, SIDES)),
            dma((2, heads, SIDES)),
            dma((far, heads)),
            dma((far, heads)),
            dma((far, heads, SIDES)),
            dma((far, heads, SIDES)),
            dma((far, heads, SIDES)),
            dma((far, heads, SIDES)),
            dma((heads,)),
            dma((heads,)),
            dma((n_grp,)),
            dma((n_grp,)),
        ],
        compiler_params=pltpu.CompilerParams(
            collective_id=0, has_side_effects=True, vmem_limit_bytes=56 * 2**20
        ),
        name="layered",
    )(streams, filters, gain.reshape(1, chans))


def passed_along(block, axis, distance):
    devices = range(lax.axis_size(axis))
    route = [(i - distance, i) for i in devices if i - distance in devices]
    return lax.ppermute(block, axis, route)


def filter_all(streams, filters):
    tok_rows = streams.shape[1]
    chan_count = streams.shape[2]
    filt_len = filters.shape[2]
    group_count = filters.shape[1]
    group_width = chan_count // group_count
    tail = streams[:, tok_rows - filt_len :, :]
    before = passed_along(tail, "ctx", 1)
    padded = jnp.concatenate([before, streams], axis=1)
    block_count = tok_rows // filt_len
    blocks = padded.reshape(3, block_count + 1, filt_len, group_count, group_width)
    zeros = jnp.zeros_like(filters)
    line = jnp.concatenate([zeros[..., :1], filters[..., ::-1], zeros], axis=2)
    table = jnp.broadcast_to(line[:, :, None, :], line.shape[:2] + (filt_len, line.shape[2]))
    table = table.reshape(3, group_count, -1)[..., : 2 * filt_len * filt_len]
    table = table.reshape(3, group_count, filt_len, 2 * filt_len)
    upper, lower = table[..., :filt_len], table[..., filt_len:]
    result = jnp.einsum(
        "agts,absgc->abtgc", lower, blocks[:, 1:], preferred_element_type=jnp.float32
    )
    result = result + jnp.einsum(
        "agts,absgc->abtgc", upper, blocks[:, :-1], preferred_element_type=jnp.float32
    )
    return result.reshape(3, tok_rows, chan_count).astype(jnp.bfloat16)


def attend(queries, positions, keyed, valued):
    tok_rows, chan_count = queries.shape
    head_count = chan_count // HD
    scale = HD ** (-0.5)
    query_heads = queries.reshape(tok_rows, head_count, HD)
    query_last = jnp.max(positions)
    start_state = (
        jnp.full((head_count, tok_rows), -1e30, jnp.float32),
        jnp.zeros((head_count, tok_rows), jnp.float32),
        jnp.zeros((tok_rows, head_count, HD), jnp.float32),
    )
    key_piece = lax.all_gather(keyed, "ctx", axis=0, tiled=True)
    value_piece = lax.all_gather(valued, "ctx", axis=0, tiled=True)
    piece_len = key_piece.shape[0]
    block_len = math.gcd(piece_len, 512)

    def step_block(step_idx, state):
        offset = step_idx * block_len
        key_block = lax.dynamic_slice_in_dim(key_piece, offset, block_len, 0).reshape(
            block_len, head_count, HD
        )
        value_block = lax.dynamic_slice_in_dim(value_piece, offset, block_len, 0).reshape(
            block_len, head_count, HD
        )
        key_pos = offset + jnp.arange(block_len, dtype=jnp.int32)

        def update_block(inner):
            running, totals, accum = inner
            scores = (
                jnp.einsum(
                    "shd,khd->hsk", query_heads, key_block, preferred_element_type=jnp.float32
                )
                * scale
            )
            causal = key_pos[None, None, :] <= positions[None, :, None]
            newtop = jnp.maximum(running, jnp.max(jnp.where(causal, scores, -1e30), axis=2))
            weights = jnp.where(causal, jnp.exp(scores - newtop[:, :, None]), 0.0)
            factor = jnp.exp(running - newtop)
            totals = totals * factor + jnp.sum(weights, axis=2)
            accum = accum * factor.T[:, :, None] + jnp.einsum(
                "hsk,khd->shd",
                weights.astype(jnp.bfloat16),
                value_block,
                preferred_element_type=jnp.float32,
            )
            return (newtop, totals, accum)

        return lax.cond(offset > query_last, lambda inner: inner, update_block, state)

    running, totals, accum = lax.fori_loop(0, piece_len // block_len, step_block, start_state)
    return (accum / totals.T[:, :, None]).reshape(tok_rows, chan_count).astype(jnp.bfloat16)


def local(streams, filters, gain):
    features = filter_all(streams, filters)
    tok_rows = streams.shape[1]
    my_index = lax.axis_index("ctx")
    queries = features[0]
    positions = my_index * tok_rows + jnp.arange(tok_rows, dtype=jnp.int32)
    attended = attend(queries, positions, features[1], features[2])
    wide = attended.astype(jnp.float32)
    power = lax.psum(jnp.sum(wide * wide, axis=1), "grp") / (streams.shape[2] * lax.axis_size("grp"))
    return (wide * gain[None, :] * lax.rsqrt(power + 1e-06)[:, None]).astype(jnp.bfloat16)


def chosen(streams, filters, gain):
    n = lax.axis_size("ctx")
    _, rows, chans = streams.shape
    _, groups, flen = filters.shape
    whole_heads = chans % (SIDES * HD) == 0
    fits = flen == LANES and rows % flen == 0 and LANES % (chans // groups) == 0
    if n == SIDES * LAYERS and whole_heads and fits:
        return layered(streams, filters, gain)
    return local(streams, filters, gain)


def solution(mesh):
    placed = (P(None, "ctx", "grp"), P(None, "grp", None), P("grp"))
    return jax.shard_map(
        chosen, mesh=mesh, in_specs=placed, out_specs=P("ctx", "grp"), check_vma=False
    )
```
